32 devices in a mesh: facet: 4 (over z), col: 8 (over y, x, core).
Axes of the slice: x: 2, y: 2, z: 4, core: 2. Of those that a mesh axis runs over, the one named last changes fastest.
Arguments:
- facets: bfloat16 [4, 64, 2, 128], P('facet', 'col'), may hold values from -6 to 6
- sub_offsets: int32 [8, 4], P('col'), may hold values from 0 to 8191
- col_offsets: int32 [8], P('col'), may hold values from 0 to 8191
- screen_index: int32 [8, 4], P('col', 'facet'), may hold values from 0 to 3
- screens: float32 [4, 2, 256, 256], replicated, may hold values from -6 to 6
Outputs:
- facets_out: float32 [4, 64, 2, 128], P('facet', 'col')
The draws below stay inside these ranges and needn't reach their ends.
All inputs are finite; a program needn't handle non-finite values.
Results may differ from the reference program's by a relative error of at most 0.0056.
Values may be sent and summed in bfloat16 or wider, within the bound.
No kernel may reach another device: no remote copies, remote signals or barrier semaphores. Data moves between devices by JAX's collectives and lax.ppermute only.
A program may use at most 64 MiB of HBM per device.

```python
import math
import jax
import jax.numpy as jnp
from jax import lax

XC = 64
XS = 256
SLAB = 128
NPAD = 8192
NSCREEN = 4
NFACET = 4
NCOL = 8
FH = 64
NSUB = 4


def touch_ends(values, own_key, smallest, high):
    place = [jax.random.randint(jax.random.fold_in(own_key, axis), (), 0, length) for axis, length in enumerate(values.shape)]
    main_axis = values.shape.index(max(values.shape))
    beside = place[:main_axis] + [(place[main_axis] + 1) % values.shape[main_axis]] + place[main_axis + 1:]
    return values.at[tuple(place)].set(smallest).at[tuple(beside)].set(high)


def shard_levels(rng, extent, split, smallest, high):
    loudness = 1.0
    for dim, blocks in split:
        draws = jax.random.uniform(jax.random.fold_in(jax.random.fold_in(rng, 6), dim), (blocks,), jnp.float32, smallest / len(split), high / len(split))
        loudness = loudness * jnp.repeat(jnp.exp(draws), extent[dim] // blocks).reshape((-1,) + (1,) * (len(extent) - 1 - dim))
    return loudness


def bell_draw(rng, dims, width, most, shards=(), kind=jnp.bfloat16):
    drawn = jax.random.normal(rng, dims, jnp.float32) * width
    if len(shards) > 0:
        drawn = shard_levels(rng, dims, shards, -0.22, 0.18) * drawn
    return jnp.clip(drawn, min=-most, max=most).astype(kind)


def setup_inputs(seed: int = 0) -> dict:
    keys = jax.random.split(jax.random.key(seed), 6)
    return {
        "facets": bell_draw(keys[0], (NFACET, FH, 2, SLAB), 1.0, 6.0, ((0, 4), (1, 8))),
        "sub_offsets": touch_ends(jax.random.randint(keys[1], (NCOL, NSUB), 0, NPAD), jax.random.fold_in(keys[1], 1), 0, NPAD - 1).astype(jnp.int32),
        "col_offsets": touch_ends(jax.random.randint(keys[2], (NCOL,), 0, NPAD), jax.random.fold_in(keys[2], 1), 0, NPAD - 1).astype(jnp.int32),
        "screen_index": touch_ends(jax.random.randint(keys[3], (NCOL, NSUB), 0, NSCREEN), jax.random.fold_in(keys[3], 1), 0, NSCREEN - 1).astype(jnp.int32),
        "screens": bell_draw(keys[4], (NSCREEN, 2, XS, XS), 1.0, 6.0, (), jnp.float32),
    }


def phase_pair(numerator, period, direction, factor):
    angles = direction * 2.0 * math.pi / period * numerator.astype(jnp.float32)
    return ((jnp.cos(angles) * factor).astype(jnp.bfloat16), (jnp.sin(angles) * factor).astype(jnp.bfloat16))

def embed_table(facet_ids):
    column = jnp.arange(XS, dtype=jnp.int32)
    within = jnp.arange(XC, dtype=jnp.int32)
    product = column[None, :, None] * (within[None, None, :] + 7 * facet_ids[:, None, None]) % XS
    return phase_pair(product, XS, 1.0, 1.0 / math.sqrt(XS))

def column_table(offset):
    position = jnp.arange(SLAB, dtype=jnp.int32)
    frequency = (offset + jnp.arange(XC, dtype=jnp.int32)) % NPAD
    product = position[:, None] * frequency[None, :] % NPAD
    return phase_pair(product, NPAD, -1.0, 1.0 / math.sqrt(SLAB))

def row_table(offsets, row_ids, height):
    frequency = (offsets[:, None] + jnp.arange(XC, dtype=jnp.int32)[None, :]) % NPAD
    frequency = frequency.reshape(frequency.shape + (1,) * row_ids.ndim)
    product = frequency * (row_ids % NPAD) % NPAD
    return phase_pair(product, NPAD, -1.0, 1.0 / math.sqrt(height))

def complex_einsum(form, first_op, second_op):
    first_real = first_op[0].astype(jnp.float32)
    first_imag = first_op[1].astype(jnp.float32)
    second_real = second_op[0].astype(jnp.float32)
    second_imag = second_op[1].astype(jnp.float32)
    real_part = jnp.einsum(form, first_real, second_real) - jnp.einsum(form, first_imag, second_imag)
    imag_part = jnp.einsum(form, first_real, second_imag) + jnp.einsum(form, first_imag, second_real)
    return (real_part, imag_part)

def round_pair(values):
    return (values[0].astype(jnp.bfloat16), values[1].astype(jnp.bfloat16))

def conjugate(values):
    return (values[0], -values[1])

def reference(facets, sub_offsets, col_offsets, screen_index, screens):
    facet_ids = jnp.arange(NFACET, dtype=jnp.int32)
    embedding = embed_table(facet_ids)
    adjoint_embed = conjugate(embedding)
    row_ids = facet_ids[:, None] * FH + jnp.arange(FH, dtype=jnp.int32)[None, :]
    facet_data = (facets[:, :, 0, :], facets[:, :, 1, :])

    def column_step(running, inputs):
        offsets, offset, screen_now = inputs
        across = column_table(offset)
        row_phase = row_table(offsets, row_ids, FH)
        spread = round_pair(complex_einsum('frx,xv->frv', facet_data, across))
        contributions = round_pair(complex_einsum('sufr,frv->fsuv', row_phase, spread))
        halfway = round_pair(complex_einsum('fsuv,fav->fsua', contributions, embedding))
        subgrid = complex_einsum('fau,fsub->sab', embedding, halfway)
        factor = 1.0 / math.sqrt(NFACET)
        sub_real = subgrid[0] * factor
        sub_imag = subgrid[1] * factor
        gain_maps = screens[screen_now]
        gain_real = gain_maps[:, 0]
        gain_imag = gain_maps[:, 1]
        screened = round_pair((sub_real * gain_real - sub_imag * gain_imag, sub_real * gain_imag + sub_imag * gain_real))
        inner = round_pair(complex_einsum('fau,sab->fsub', adjoint_embed, screened))
        returned = round_pair(complex_einsum('fsub,fbv->fsuv', inner, adjoint_embed))
        slab_rows = round_pair(complex_einsum('sufr,fsuv->frv', conjugate(row_phase), returned))
        summand = complex_einsum('frv,xv->frx', slab_rows, conjugate(across))
        return ((running[0] + summand[0], running[1] + summand[1]), None)
    empty_sum = jnp.zeros((NFACET, FH, SLAB), jnp.float32)
    running, _ = lax.scan(column_step, (empty_sum, empty_sum), (sub_offsets, col_offsets, screen_index))
    factor = 1.0 / math.sqrt(NCOL * NSUB)
    return jnp.stack([running[0] * factor, running[1] * factor], axis=2)
```

```python
import functools
import math

import jax
import jax.numpy as jnp
from jax import lax
from jax.experimental import pallas as pl
from jax.experimental.pallas import tpu as pltpu
from jax.sharding import PartitionSpec as P

XC = 64
NPAD = 8192
STEP = 7
LANES = 128
CHUNK = 256
F32 = jnp.float32
BF16 = jnp.bfloat16
VMEM = pltpu.MemorySpace.VMEM


def wave(number, period, scale):
    quarter = period // 4
    bits = quarter.bit_length() - 1
    turn = (number + quarter // 2) >> bits
    angle = (number - (turn << bits)).astype(F32) * (2.0 * math.pi / period)
    square = angle * angle
    sine = angle * (1.0 + square * (-1 / 6 + square * (1 / 120 + square * (-1 / 5040))))
    cosine = 1.0 + square * (-1 / 2 + square * (1 / 24 + square * (-1 / 720 + square * (1 / 40320))))
    odd = (turn & 1) == 1
    first = jnp.where(odd, sine, cosine)
    second = jnp.where(odd, cosine, sine)
    first = jnp.where(((turn + 1) & 2) == 2, -scale, scale) * first
    second = jnp.where((turn & 2) == 2, -scale, scale) * second
    return first, second


def each(count, step):
    if count == 1:
        step(0)
    else:
        lax.fori_loop(0, count, lambda i, c: (step(i), c)[1], 0)


def iota(shape, axis):
    return lax.broadcasted_iota(jnp.int32, shape, axis)


def tables_kernel(
    dims, col_ref, sub_ref, pick_ref, screens_ref,
    a_ref, p_ref, w_ref, wt_ref, wc_ref, wh_ref, ph_ref, ah_ref, gain_ref, sem,
):
    facets, height, span, slab, size, owned, chunk = dims
    rows = facets * height
    copies = [
        pltpu.make_async_copy(screens_ref.at[pick_ref[k]], gain_ref.at[k], sem.at[k])
        for k in range(owned)
    ]
    for copy in copies:
        copy.start()
    shift = height.bit_length() - 1

    def phases(p, row, offset):
        u = p - STEP * (row >> shift)
        frequency = (offset + u) & (NPAD - 1)
        number = (frequency * (row & (NPAD - 1))) & (NPAD - 1)
        inside = (u >= 0) & (u < XC)
        real, imag = wave(number, NPAD, 1.0 / math.sqrt(height))
        zero = jnp.zeros_like(real)
        return jnp.where(inside, real, zero).astype(BF16), jnp.where(inside, -imag, zero).astype(BF16)

    def row_chunk(k, i):
        base = i * chunk
        along = pl.ds(pl.multiple_of(base, chunk), chunk) if not isinstance(i, int) else pl.ds(base, chunk)
        shape = (span, chunk)
        real, imag = phases(iota(shape, 0), iota(shape, 1) + base, sub_ref[k])
        p_ref[k, :span, along] = real
        p_ref[k, span:, along] = imag
        shape = (chunk, span)
        real, imag = phases(iota(shape, 1), iota(shape, 0) + base, sub_ref[k])
        ph_ref[k, along, :span] = real
        ph_ref[k, along, span:] = imag

    for k in range(owned):
        each(rows // chunk, functools.partial(row_chunk, k))

    def across(x, v):
        frequency = (col_ref[0] + v) & (NPAD - 1)
        number = (x * frequency) & (NPAD - 1)
        real, imag = wave(number, NPAD, 1.0 / math.sqrt(slab))
        zero = jnp.zeros_like(real)
        inside = v < XC
        return jnp.where(inside, real, zero).astype(BF16), jnp.where(inside, -imag, zero).astype(BF16)

    shape = (slab, span)
    real, imag = across(iota(shape, 0), iota(shape, 1))
    a_ref[:slab, :span] = real
    a_ref[:slab, span:] = imag
    a_ref[slab:, :span] = -imag
    a_ref[slab:, span:] = real
    shape = (span, slab)
    real, imag = across(iota(shape, 1), iota(shape, 0))
    ah_ref[:span, :slab] = real
    ah_ref[:span, slab:] = -imag
    ah_ref[span:, :slab] = imag
    ah_ref[span:, slab:] = real

    scale = 1.0 / math.sqrt(size)
    shape = (size, span)
    real, imag = wave((iota(shape, 0) * iota(shape, 1)) & (size - 1), size, scale)
    real, imag = real.astype(BF16), imag.astype(BF16)
    w_ref[:, :span] = real
    w_ref[:, span:] = imag
    wc_ref[:size, :span] = real
    wc_ref[:size, span:] = -imag
    wc_ref[size:, :span] = imag
    wc_ref[size:, span:] = real
    shape = (span, size)
    real, imag = wave((iota(shape, 0) * iota(shape, 1)) & (size - 1), size, scale)
    wh_ref[:span, :] = real.astype(BF16)
    wh_ref[span:, :] = imag.astype(BF16)
    factor = 1.0 / math.sqrt(facets)
    real, imag = (real * factor).astype(BF16), (imag * factor).astype(BF16)
    wt_ref[:span, :size] = real
    wt_ref[:span, size:] = imag
    wt_ref[span:, :size] = -imag
    wt_ref[span:, size:] = real
    for copy in copies:
        copy.wait()


def dot(first, second):
    return jnp.dot(first, second, preferred_element_type=F32)


def main_kernel(
    dims, x_ref, a_ref, p_ref, w_ref, wt_ref, wc_ref, wh_ref, ph_ref, ah_ref, gain_ref, out_ref,
    spread_ref,
):
    facets, height, span, slab, size, owned, chunk = dims
    rows = facets * height

    def turned(block, base, sign):
        parts = []
        for i in range(block.shape[0] // height):
            amount = STEP * (base + i)
            if isinstance(amount, int) and amount == 0:
                parts.append(block[i * height : (i + 1) * height].astype(BF16))
                continue
            amount = amount if sign > 0 else span - amount
            piece = block[i * height : (i + 1) * height]
            halves = [pltpu.roll(piece[:, h * span : (h + 1) * span], amount, 1) for h in (0, 1)]
            parts.append(jnp.concatenate(halves, axis=1).astype(BF16))
        return parts[0] if len(parts) == 1 else jnp.concatenate(parts, axis=0)

    def along(i):
        return pl.ds(i * chunk, chunk) if isinstance(i, int) else pl.ds(pl.multiple_of(i * chunk, chunk), chunk)

    def spread(i):
        block = dot(x_ref[along(i), :], a_ref[...])
        spread_ref[along(i), :] = turned(block, i * (chunk // height), 1)

    each(rows // chunk, spread)
    total = []
    for k in range(owned):
        quad = dot(p_ref[k], spread_ref[...])
        real = (quad[:span, :span] - quad[span:, span:]).astype(BF16)
        imag = (quad[:span, span:] + quad[span:, :span]).astype(BF16)
        both = jnp.concatenate(
            [jnp.concatenate([real, imag], axis=1), jnp.concatenate([-imag, real], axis=1)], axis=0
        )
        half = dot(w_ref[...], both).astype(BF16)
        grid = dot(half, wt_ref[...])
        real, imag = grid[:, :size], grid[:, size:]
        gain_real, gain_imag = gain_ref[k, 0], gain_ref[k, 1]
        seen = jnp.concatenate(
            [
                (real * gain_real - imag * gain_imag).astype(BF16),
                (real * gain_imag + imag * gain_real).astype(BF16),
            ],
            axis=1,
        )
        inner = dot(seen, wc_ref[...]).astype(BF16)
        quad = dot(wh_ref[...], inner)
        real = (quad[:span, :span] + quad[span:, span:]).astype(BF16)
        imag = (quad[:span, span:] - quad[span:, :span]).astype(BF16)
        total.append(
            jnp.concatenate(
                [jnp.concatenate([real, imag], axis=1), jnp.concatenate([imag, -real], axis=1)], axis=0
            )
        )

    def back(i):
        block = dot(ph_ref[0, along(i), :], total[0])
        for k in range(1, owned):
            block += dot(ph_ref[k, along(i), :], total[k])
        out_ref[along(i), :] = dot(turned(block, i * (chunk // height), -1), ah_ref[...]).astype(BF16)

    each(rows // chunk, back)


def whole(count):
    return [pl.BlockSpec(memory_space=VMEM)] * count


def body(facets, sub_offsets, col_offsets, screen_index, screens):
    axes = ("facet", "col")
    facet_now = lax.axis_index("facet")
    facet_count = lax.axis_size("facet")
    column_count = lax.axis_size("col")
    devices = facet_count * column_count
    local_rows, slab = facets.shape[1], facets.shape[3]
    height = local_rows * column_count
    rows = facet_count * height
    subgrid_count = sub_offsets.shape[1]
    owned = subgrid_count // facet_count
    size = screens.shape[2]
    span = -(-(XC + STEP * (facet_count - 1)) // LANES) * LANES
    chunk = max(height, min(rows, CHUNK))
    dims = (facet_count, height, span, slab, size, owned, chunk)

    mine = facets[0].reshape(local_rows, 2 * slab)
    everyone = lax.all_to_all(
        jnp.tile(mine, (devices, 1)), axes, split_axis=0, concat_axis=0, tiled=True
    )
    own_offsets = lax.dynamic_slice(sub_offsets[0], (facet_now * owned,), (owned,))
    table_shapes = [
        ((2 * slab, 2 * span), BF16),
        ((owned, 2 * span, rows), BF16),
        ((size, 2 * span), BF16),
        ((2 * span, 2 * size), BF16),
        ((2 * size, 2 * span), BF16),
        ((2 * span, size), BF16),
        ((owned, rows, 2 * span), BF16),
        ((2 * span, 2 * slab), BF16),
        ((owned, 2, size, size), F32),
    ]
    table_bytes = sum(math.prod(s) * jnp.dtype(t).itemsize for s, t in table_shapes)
    tables = pl.pallas_call(
        functools.partial(tables_kernel, dims),
        out_shape=[jax.ShapeDtypeStruct(s, t) for s, t in table_shapes],
        in_specs=[pl.BlockSpec(memory_space=pltpu.MemorySpace.SMEM)] * 3
        + [pl.BlockSpec(memory_space=pl.ANY)],
        out_specs=whole(len(table_shapes)),
        scratch_shapes=[pltpu.SemaphoreType.DMA((owned,))],
        cost_estimate=pl.CostEstimate(
            flops=100 * table_bytes, bytes_accessed=2 * table_bytes, transcendentals=0
        ),
        name="tables",
    )(col_offsets, own_offsets, screen_index[0], screens)
    terms = pl.pallas_call(
        functools.partial(main_kernel, dims),
        out_shape=jax.ShapeDtypeStruct((rows, 2 * slab), BF16),
        in_specs=whole(1 + len(tables)),
        out_specs=pl.BlockSpec(memory_space=VMEM),
        scratch_shapes=[pltpu.VMEM((rows, 2 * span), BF16)],
        name="window",
    )(everyone, *tables)
    arrived = lax.all_to_all(terms, axes, split_axis=0, concat_axis=0, tiled=True)
    factor = 1.0 / math.sqrt(column_count * subgrid_count)
    summed = jnp.sum(arrived.reshape(devices, local_rows, 2 * slab).astype(F32), axis=0) * factor
    return summed.reshape(1, local_rows, 2, slab)


def solution(mesh):
    return jax.shard_map(
        body,
        mesh=mesh,
        in_specs=(P("facet", "col", None, None), P("col", None), P("col"), P("col", "facet"), P()),
        out_specs=P("facet", "col", None, None),
        check_vma=False,
    )
```

```python
import functools
import math

import jax
import jax.numpy as jnp
from jax import lax
from jax.experimental import pallas as pl
from jax.experimental.pallas import tpu as pltpu
from jax.sharding import PartitionSpec as P

XC = 64
NPAD = 8192
STEP = 7
LANES = 128
CHUNK = 256
VMEM_LIMIT = 24 * 2**20
F32 = jnp.float32
BF16 = jnp.bfloat16
VMEM = pltpu.MemorySpace.VMEM


def wave(number, period, scale):
    quarter = period // 4
    bits = quarter.bit_length() - 1
    turn = (number + quarter // 2) >> bits
    angle = (number - (turn << bits)).astype(F32) * (2.0 * math.pi / period)
    square = angle * angle
    sine = angle * (1.0 + square * (-1 / 6 + square * (1 / 120 + square * (-1 / 5040))))
    cosine = 1.0 + square * (-1 / 2 + square * (1 / 24 + square * (-1 / 720 + square * (1 / 40320))))
    odd = (turn & 1) == 1
    first = jnp.where(odd, sine, cosine)
    second = jnp.where(odd, cosine, sine)
    first = jnp.where(((turn + 1) & 2) == 2, -scale, scale) * first
    second = jnp.where((turn & 2) == 2, -scale, scale) * second
    return first, second


def each(count, step):
    if count == 1:
        step(0)
    else:
        lax.fori_loop(0, count, lambda i, c: (step(i), c)[1], 0)


def iota(shape, axis):
    return lax.broadcasted_iota(jnp.int32, shape, axis)


def tables_kernel(
    dims, numbers_hbm, screens_ref,
    a_ref, p_ref, w_ref, wt_ref, wc_ref, wh_ref, ph_ref, ah_ref, gain_ref,
    numbers_ref, small_sem, sem,
):
    facets, height, span, slab, size, owned, chunk = dims
    rows = facets * height
    small = pltpu.make_async_copy(numbers_hbm, numbers_ref, small_sem)
    small.start()

    scale = 1.0 / math.sqrt(size)
    shape = (size, span)
    real, imag = wave((iota(shape, 0) * iota(shape, 1)) & (size - 1), size, scale)
    real, imag = real.astype(BF16), imag.astype(BF16)
    w_ref[:, :span] = real
    w_ref[:, span:] = imag
    wc_ref[:size, :span] = real
    wc_ref[:size, span:] = -imag
    wc_ref[size:, :span] = imag
    wc_ref[size:, span:] = real
    shape = (span, size)
    real, imag = wave((iota(shape, 0) * iota(shape, 1)) & (size - 1), size, scale)
    wh_ref[:span, :] = real.astype(BF16)
    wh_ref[span:, :] = imag.astype(BF16)
    factor = 1.0 / math.sqrt(facets)
    real, imag = (real * factor).astype(BF16), (imag * factor).astype(BF16)
    wt_ref[:span, :size] = real
    wt_ref[:span, size:] = imag
    wt_ref[span:, :size] = -imag
    wt_ref[span:, size:] = real

    small.wait()
    copies = [
        pltpu.make_async_copy(screens_ref.at[numbers_ref[1 + k]], gain_ref.at[k], sem.at[k])
        for k in range(owned)
    ]
    for copy in copies:
        copy.start()
    first = 1 + owned + lax.axis_index("facet") * owned
    shift = height.bit_length() - 1

    def phases(p, row, offset):
        u = p - STEP * (row >> shift)
        frequency = (offset + u) & (NPAD - 1)
        number = (frequency * (row & (NPAD - 1))) & (NPAD - 1)
        inside = (u >= 0) & (u < XC)
        real, imag = wave(number, NPAD, 1.0 / math.sqrt(height))
        zero = jnp.zeros_like(real)
        return jnp.where(inside, real, zero).astype(BF16), jnp.where(inside, -imag, zero).astype(BF16)

    def row_chunk(k, i):
        base = i * chunk
        along = pl.ds(pl.multiple_of(base, chunk), chunk) if not isinstance(i, int) else pl.ds(base, chunk)
        shape = (span, chunk)
        real, imag = phases(iota(shape, 0), iota(shape, 1) + base, numbers_ref[first + k])
        p_ref[k, :span, along] = real
        p_ref[k, span:, along] = imag
        shape = (chunk, span)
        real, imag = phases(iota(shape, 1), iota(shape, 0) + base, numbers_ref[first + k])
        ph_ref[k, along, :span] = real
        ph_ref[k, along, span:] = imag

    for k in range(owned):
        each(rows // chunk, functools.partial(row_chunk, k))

    def across(x, v):
        frequency = (numbers_ref[0] + v) & (NPAD - 1)
        number = (x * frequency) & (NPAD - 1)
        real, imag = wave(number, NPAD, 1.0 / math.sqrt(slab))
        zero = jnp.zeros_like(real)
        inside = v < XC
        return jnp.where(inside, real, zero).astype(BF16), jnp.where(inside, -imag, zero).astype(BF16)

    shape = (slab, span)
    real, imag = across(iota(shape, 0), iota(shape, 1))
    a_ref[:slab, :span] = real
    a_ref[:slab, span:] = imag
    a_ref[slab:, :span] = -imag
    a_ref[slab:, span:] = real
    shape = (span, slab)
    real, imag = across(iota(shape, 1), iota(shape, 0))
    ah_ref[:span, :slab] = real
    ah_ref[:span, slab:] = -imag
    ah_ref[span:, :slab] = imag
    ah_ref[span:, slab:] = real

    for copy in copies:
        copy.wait()


def dot(first, second):
    return jnp.dot(first, second, preferred_element_type=F32)


def main_kernel(
    dims, x_ref, a_ref, p_ref, w_ref, wt_ref, wc_ref, wh_ref, ph_ref, ah_ref, gain_ref, out_ref,
    spread_ref,
):
    facets, height, span, slab, size, owned, chunk = dims
    rows = facets * height

    def turned(block, base, sign):
        parts = []
        for i in range(block.shape[0] // height):
            amount = STEP * (base + i)
            if isinstance(amount, int) and amount == 0:
                parts.append(block[i * height : (i + 1) * height].astype(BF16))
                continue
            amount = amount if sign > 0 else span - amount
            piece = block[i * height : (i + 1) * height]
            halves = [pltpu.roll(piece[:, h * span : (h + 1) * span], amount, 1) for h in (0, 1)]
            parts.append(jnp.concatenate(halves, axis=1).astype(BF16))
        return parts[0] if len(parts) == 1 else jnp.concatenate(parts, axis=0)

    def along(i):
        return pl.ds(i * chunk, chunk) if isinstance(i, int) else pl.ds(pl.multiple_of(i * chunk, chunk), chunk)

    def spread(i):
        block = dot(x_ref[along(i), :], a_ref[...])
        spread_ref[along(i), :] = turned(block, i * (chunk // height), 1)

    each(rows // chunk, spread)
    total = []
    for k in range(owned):
        quad = dot(p_ref[k], spread_ref[...])
        real = (quad[:span, :span] - quad[span:, span:]).astype(BF16)
        imag = (quad[:span, span:] + quad[span:, :span]).astype(BF16)
        both = jnp.concatenate(
            [jnp.concatenate([real, imag], axis=1), jnp.concatenate([-imag, real], axis=1)], axis=0
        )
        half = dot(w_ref[...], both).astype(BF16)
        grid = dot(half, wt_ref[...])
        real, imag = grid[:, :size], grid[:, size:]
        gain_real, gain_imag = gain_ref[k, 0], gain_ref[k, 1]
        seen = jnp.concatenate(
            [
                (real * gain_real - imag * gain_imag).astype(BF16),
                (real * gain_imag + imag * gain_real).astype(BF16),
            ],
            axis=1,
        )
        inner = dot(seen, wc_ref[...]).astype(BF16)
        quad = dot(wh_ref[...], inner)
        real = (quad[:span, :span] + quad[span:, span:]).astype(BF16)
        imag = (quad[:span, span:] - quad[span:, :span]).astype(BF16)
        total.append(
            jnp.concatenate(
                [jnp.concatenate([real, imag], axis=1), jnp.concatenate([imag, -real], axis=1)], axis=0
            )
        )

    def back(i):
        block = dot(ph_ref[0, along(i), :], total[0])
        for k in range(1, owned):
            block += dot(ph_ref[k, along(i), :], total[k])
        out_ref[along(i), :] = dot(turned(block, i * (chunk // height), -1), ah_ref[...]).astype(BF16)

    each(rows // chunk, back)


def send_kernel(facets_ref, out_ref, mine_ref, sem):
    copy = pltpu.make_async_copy(facets_ref, mine_ref, sem)
    copy.start()
    copy.wait()
    mine = jnp.concatenate([mine_ref[0, :, 0, :], mine_ref[0, :, 1, :]], axis=1)
    out_ref[...] = jnp.broadcast_to(mine[None], out_ref.shape)


def in_hbm(array):
    return pltpu.with_memory_space_constraint(array, pltpu.MemorySpace.HBM)


def whole(count):
    return [pl.BlockSpec(memory_space=VMEM)] * count


def body(facets, sub_offsets, col_offsets, screen_index, screens):
    axes = ("facet", "col")
    facet_count = lax.axis_size("facet")
    column_count = lax.axis_size("col")
    devices = facet_count * column_count
    local_rows, slab = facets.shape[1], facets.shape[3]
    height = local_rows * column_count
    rows = facet_count * height
    subgrid_count = sub_offsets.shape[1]
    owned = subgrid_count // facet_count
    size = screens.shape[2]
    span = -(-(XC + STEP * (facet_count - 1)) // LANES) * LANES
    chunk = max(height, min(rows, CHUNK))
    dims = (facet_count, height, span, slab, size, owned, chunk)

    outgoing = pl.pallas_call(
        send_kernel,
        out_shape=jax.ShapeDtypeStruct((devices, local_rows, 2 * slab), BF16),
        in_specs=[pl.BlockSpec(memory_space=pl.ANY)],
        out_specs=pl.BlockSpec(memory_space=VMEM),
        scratch_shapes=[pltpu.VMEM(facets.shape, BF16), pltpu.SemaphoreType.DMA],
        compiler_params=pltpu.CompilerParams(vmem_limit_bytes=VMEM_LIMIT),
        name="send",
    )(in_hbm(facets))
    everyone = lax.all_to_all(outgoing, axes, split_axis=0, concat_axis=0, tiled=True)
    everyone = everyone.reshape(rows, 2 * slab)
    numbers = jnp.concatenate([col_offsets, screen_index[0], sub_offsets[0]])
    table_shapes = [
        ((2 * slab, 2 * span), BF16),
        ((owned, 2 * span, rows), BF16),
        ((size, 2 * span), BF16),
        ((2 * span, 2 * size), BF16),
        ((2 * size, 2 * span), BF16),
        ((2 * span, size), BF16),
        ((owned, rows, 2 * span), BF16),
        ((2 * span, 2 * slab), BF16),
        ((owned, 2, size, size), F32),
    ]
    table_bytes = sum(math.prod(s) * jnp.dtype(t).itemsize for s, t in table_shapes)
    tables = pl.pallas_call(
        functools.partial(tables_kernel, dims),
        out_shape=[jax.ShapeDtypeStruct(s, t) for s, t in table_shapes],
        in_specs=[pl.BlockSpec(memory_space=pl.ANY)] * 2,
        out_specs=whole(len(table_shapes)),
        scratch_shapes=[
            pltpu.SMEM(numbers.shape, jnp.int32),
            pltpu.SemaphoreType.DMA,
            pltpu.SemaphoreType.DMA((owned,)),
        ],
        compiler_params=pltpu.CompilerParams(vmem_limit_bytes=VMEM_LIMIT),
        cost_estimate=pl.CostEstimate(
            flops=100 * table_bytes, bytes_accessed=2 * table_bytes, transcendentals=0
        ),
        name="tables",
    )(numbers, in_hbm(screens))
    terms = pl.pallas_call(
        functools.partial(main_kernel, dims),
        out_shape=jax.ShapeDtypeStruct((rows, 2 * slab), BF16),
        in_specs=whole(1 + len(tables)),
        out_specs=pl.BlockSpec(memory_space=VMEM),
        scratch_shapes=[pltpu.VMEM((rows, 2 * span), BF16)],
        compiler_params=pltpu.CompilerParams(vmem_limit_bytes=VMEM_LIMIT),
        name="window",
    )(everyone, *tables)
    terms = terms.reshape(devices, local_rows, 2 * slab)
    arrived = lax.all_to_all(terms, axes, split_axis=0, concat_axis=0, tiled=True)
    factor = 1.0 / math.sqrt(column_count * subgrid_count)
    summed = jnp.sum(arrived.astype(F32), axis=0) * factor
    return summed.reshape(1, local_rows, 2, slab)


def solution(mesh):
    return jax.shard_map(
        body,
        mesh=mesh,
        in_specs=(P("facet", "col", None, None), P("col", None), P("col"), P("col", "facet"), P()),
        out_specs=P("facet", "col", None, None),
        check_vma=False,
    )
```

```python
import functools
import math

import jax
import jax.numpy as jnp
from jax import lax
from jax.experimental import pallas as pl
from jax.experimental.pallas import tpu as pltpu
from jax.sharding import PartitionSpec as P

XC = 64
NPAD = 8192
STEP = 7
ROWS = 8
LANES = 128
CHUNK = 256
VMEM_LIMIT = 24 * 2**20
F32 = jnp.float32
BF16 = jnp.bfloat16
VMEM = pltpu.MemorySpace.VMEM


def wave(number, period, scale):
    quarter = period // 4
    bits = quarter.bit_length() - 1
    turn = (number + quarter // 2) >> bits
    angle = (number - (turn << bits)).astype(F32) * (2.0 * math.pi / period)
    square = angle * angle
    sine = angle * (1.0 + square * (-1 / 6 + square * (1 / 120 + square * (-1 / 5040))))
    cosine = 1.0 + square * (-1 / 2 + square * (1 / 24 + square * (-1 / 720 + square * (1 / 40320))))
    odd = (turn & 1) == 1
    first = jnp.where(odd, sine, cosine)
    second = jnp.where(odd, cosine, sine)
    first = jnp.where(((turn + 1) & 2) == 2, -scale, scale) * first
    second = jnp.where((turn & 2) == 2, -scale, scale) * second
    return first, second


def each(count, step):
    if count == 1:
        step(0)
    else:
        lax.fori_loop(0, count, lambda i, c: (step(i), c)[1], 0)


def iota(shape, axis):
    return lax.broadcasted_iota(jnp.int32, shape, axis)


def ladder(first, step, count):
    real, imag = first
    reals, imags = [real], [imag]
    for _ in range(count - 1):
        real, imag = real * step[0] - imag * step[1], real * step[1] + imag * step[0]
        reals.append(real)
        imags.append(imag)
    return jnp.concatenate(reals, axis=0), jnp.concatenate(imags, axis=0)


def fourier(rows, row_start, lane_numbers, period, scale):
    shape = (ROWS, lane_numbers.shape[1])
    lanes = jnp.broadcast_to(lane_numbers, shape) & (period - 1)
    top = (iota(shape, 0) + row_start) & (period - 1)
    first = wave((top * lanes) & (period - 1), period, scale)
    return ladder(first, wave((ROWS * lanes) & (period - 1), period, 1.0), rows // ROWS)


def block(real, imag, flip):
    low, high = (imag, -imag) if flip else (-imag, imag)
    return jnp.concatenate(
        [jnp.concatenate([real, high], axis=1), jnp.concatenate([low, real], axis=1)], axis=0
    )


def tables_kernel(
    dims, numbers_hbm, screens_ref,
    a_ref, wp_ref, wt_ref, w_ref, wph_ref, ah_ref, gain_ref,
    numbers_ref, small_sem, sem,
):
    facets, height, span, slab, size, owned, chunk = dims
    rows = facets * height
    small = pltpu.make_async_copy(numbers_hbm, numbers_ref, small_sem)
    small.start()

    scale = 1.0 / math.sqrt(size)
    real, imag = fourier(size, 0, iota((1, span), 1), size, scale)
    w_real, w_imag = real.astype(BF16), imag.astype(BF16)
    w_both = jnp.concatenate([w_real, w_imag], axis=1)
    w_ref[...] = w_both
    real, imag = fourier(span, 0, iota((1, size), 1), size, scale)
    wt_ref[...] = block(real.astype(BF16), imag.astype(BF16), False)

    small.wait()
    copies = [
        pltpu.make_async_copy(screens_ref.at[numbers_ref[1 + k]], gain_ref.at[k], sem.at[k])
        for k in range(owned)
    ]
    for copy in copies:
        copy.start()
    column = numbers_ref[0]

    def facet_tables(f):
        lag = STEP * f
        lanes = iota((1, span), 1) - lag
        scale = 1.0 / math.sqrt(slab)
        real, imag = fourier(slab, 0, column + lanes, NPAD, scale / math.sqrt(facets))
        inside = jnp.broadcast_to((lanes >= 0) & (lanes < XC), real.shape)
        zero = jnp.zeros_like(real)
        a_ref[f] = block(
            jnp.where(inside, real, zero).astype(BF16),
            jnp.where(inside, -imag, zero).astype(BF16),
            False,
        )
        real, imag = fourier(span, column - lag, iota((1, slab), 1), NPAD, scale)
        down = iota(real.shape, 0) - lag
        inside = (down >= 0) & (down < XC)
        zero = jnp.zeros_like(real)
        ah_ref[f] = block(
            jnp.where(inside, real, zero).astype(BF16),
            jnp.where(inside, -imag, zero).astype(BF16),
            True,
        )

    if rows == chunk:
        for f in range(facets):
            facet_tables(f)
    else:
        each(facets, facet_tables)

    first = 1 + owned + lax.axis_index("facet") * owned
    scale = 1.0 / math.sqrt(height)
    shift = height.bit_length() - 1

    def row_chunk(k, i):
        fixed = isinstance(i, int)
        base = i * chunk

        def along(start):
            return pl.ds(start, chunk) if fixed else pl.ds(pl.multiple_of(start, chunk), chunk)

        offset = numbers_ref[first + k]
        row = iota((1, chunk), 1) + base
        lag = STEP * (row >> shift)
        low = jnp.broadcast_to((offset - lag) & (NPAD - 1), (ROWS, chunk))
        lanes = jnp.broadcast_to(row & (NPAD - 1), (ROWS, chunk))
        top = (low + iota((ROWS, chunk), 0)) & (NPAD - 1)
        real, imag = ladder(
            wave((top * lanes) & (NPAD - 1), NPAD, scale),
            wave((ROWS * lanes) & (NPAD - 1), NPAD, 1.0),
            span // ROWS,
        )
        u = iota((span, chunk), 0) - lag
        inside = (u >= 0) & (u < XC)
        zero = jnp.zeros_like(real)
        real = jnp.where(inside, real, zero).astype(BF16)
        imag = jnp.where(inside, -imag, zero).astype(BF16)
        both = dot(w_both, block(real, imag, False)).astype(BF16)
        wp_ref[k, :size, along(base)] = both[:, :chunk]
        wp_ref[k, size:, along(base)] = both[:, chunk:]
        reals, imags = [], []
        for f in range(chunk // height):
            lag = STEP * ((base >> shift) + f)
            lanes = iota((1, span), 1) - lag
            real, imag = fourier(height, base + f * height, lanes + offset, NPAD, scale)
            inside = jnp.broadcast_to((lanes >= 0) & (lanes < XC), real.shape)
            zero = jnp.zeros_like(real)
            reals.append(jnp.where(inside, real, zero).astype(BF16))
            imags.append(jnp.where(inside, -imag, zero).astype(BF16))
        both = jnp.concatenate(
            [jnp.concatenate(reals, axis=0), jnp.concatenate(imags, axis=0)], axis=1
        )
        wph_ref[k, along(base), :] = dot(both, wt_ref[...]).astype(BF16)

    for k in range(owned):
        each(rows // chunk, functools.partial(row_chunk, k))
    for copy in copies:
        copy.wait()


def dot(first, second):
    return jnp.dot(first, second, preferred_element_type=F32)


def main_kernel(
    dims, x_ref, a_ref, wp_ref, wt_ref, w_ref, wph_ref, ah_ref, gain_ref, out_ref, spread_ref,
):
    facets, height, span, slab, size, owned, chunk = dims
    rows = facets * height

    def by_facet(value, i, table_ref):
        parts = []
        for f in range(chunk // height):
            own = value[f * height : (f + 1) * height]
            parts.append(dot(own, table_ref[i * (chunk // height) + f]).astype(BF16))
        return parts[0] if len(parts) == 1 else jnp.concatenate(parts, axis=0)

    def along(i):
        base = i * chunk
        return pl.ds(base, chunk) if isinstance(i, int) else pl.ds(pl.multiple_of(base, chunk), chunk)

    def spread(i):
        spread_ref[along(i), :] = by_facet(x_ref[along(i), :], i, a_ref)

    each(rows // chunk, spread)
    inners = []
    for k in range(owned):
        first = dot(wp_ref[k, :size], spread_ref[...])
        second = dot(wp_ref[k, size:], spread_ref[...])
        half = jnp.concatenate(
            [first[:, :span] - second[:, span:], first[:, span:] + second[:, :span]], axis=1
        ).astype(BF16)
        grid = dot(half, wt_ref[...])
        real, imag = grid[:, :size], grid[:, size:]
        gain_real, gain_imag = gain_ref[k, 0], gain_ref[k, 1]
        seen_real = (real * gain_real - imag * gain_imag).astype(BF16)
        seen_imag = (real * gain_imag + imag * gain_real).astype(BF16)
        first = dot(seen_real, w_ref[...])
        second = dot(seen_imag, w_ref[...])
        inners.append(
            jnp.concatenate(
                [first[:, :span] + second[:, span:], second[:, :span] - first[:, span:]], axis=1
            ).astype(BF16)
        )

    def back(i):
        own = 0.0
        for k in range(owned):
            first = dot(wph_ref[k, along(i), :size], inners[k])
            second = dot(wph_ref[k, along(i), size:], inners[k])
            own += jnp.concatenate(
                [first[:, :span] + second[:, span:], first[:, span:] - second[:, :span]], axis=1
            )
        out_ref[along(i), :] = by_facet(own.astype(BF16), i, ah_ref)

    each(rows // chunk, back)


def send_kernel(facets_ref, out_ref, mine_ref, sem):
    copy = pltpu.make_async_copy(facets_ref, mine_ref, sem)
    copy.start()
    copy.wait()
    mine = jnp.concatenate([mine_ref[0, :, 0, :], mine_ref[0, :, 1, :]], axis=1)
    out_ref[...] = jnp.broadcast_to(mine[None], out_ref.shape)


def in_hbm(array):
    return pltpu.with_memory_space_constraint(array, pltpu.MemorySpace.HBM)


def whole(count):
    return [pl.BlockSpec(memory_space=VMEM)] * count


def body(facets, sub_offsets, col_offsets, screen_index, screens):
    axes = ("facet", "col")
    facet_count = lax.axis_size("facet")
    column_count = lax.axis_size("col")
    devices = facet_count * column_count
    local_rows, slab = facets.shape[1], facets.shape[3]
    height = local_rows * column_count
    rows = facet_count * height
    subgrid_count = sub_offsets.shape[1]
    owned = subgrid_count // facet_count
    size = screens.shape[2]
    span = -(-(XC + STEP * (facet_count - 1)) // LANES) * LANES
    chunk = max(height, min(rows, CHUNK))
    dims = (facet_count, height, span, slab, size, owned, chunk)

    outgoing = pl.pallas_call(
        send_kernel,
        out_shape=jax.ShapeDtypeStruct((devices, local_rows, 2 * slab), BF16),
        in_specs=[pl.BlockSpec(memory_space=pl.ANY)],
        out_specs=pl.BlockSpec(memory_space=VMEM),
        scratch_shapes=[pltpu.VMEM(facets.shape, BF16), pltpu.SemaphoreType.DMA],
        compiler_params=pltpu.CompilerParams(vmem_limit_bytes=VMEM_LIMIT),
        name="send",
    )(in_hbm(facets))
    everyone = lax.all_to_all(outgoing, axes, split_axis=0, concat_axis=0, tiled=True)
    everyone = everyone.reshape(rows, 2 * slab)
    numbers = jnp.concatenate([col_offsets, screen_index[0], sub_offsets[0]])
    table_shapes = [
        ((facet_count, 2 * slab, 2 * span), BF16),
        ((owned, 2 * size, rows), BF16),
        ((2 * span, 2 * size), BF16),
        ((size, 2 * span), BF16),
        ((owned, rows, 2 * size), BF16),
        ((facet_count, 2 * span, 2 * slab), BF16),
        ((owned, 2, size, size), F32),
    ]
    table_bytes = sum(math.prod(s) * jnp.dtype(t).itemsize for s, t in table_shapes)
    tables = pl.pallas_call(
        functools.partial(tables_kernel, dims),
        out_shape=[jax.ShapeDtypeStruct(s, t) for s, t in table_shapes],
        in_specs=[pl.BlockSpec(memory_space=pl.ANY)] * 2,
        out_specs=whole(len(table_shapes)),
        scratch_shapes=[
            pltpu.SMEM(numbers.shape, jnp.int32),
            pltpu.SemaphoreType.DMA,
            pltpu.SemaphoreType.DMA((owned,)),
        ],
        compiler_params=pltpu.CompilerParams(vmem_limit_bytes=VMEM_LIMIT),
        cost_estimate=pl.CostEstimate(
            flops=100 * table_bytes, bytes_accessed=2 * table_bytes, transcendentals=0
        ),
        name="tables",
    )(numbers, in_hbm(screens))
    terms = pl.pallas_call(
        functools.partial(main_kernel, dims),
        out_shape=jax.ShapeDtypeStruct((rows, 2 * slab), BF16),
        in_specs=whole(1 + len(tables)),
        out_specs=pl.BlockSpec(memory_space=VMEM),
        scratch_shapes=[pltpu.VMEM((rows, 2 * span), BF16)],
        compiler_params=pltpu.CompilerParams(vmem_limit_bytes=VMEM_LIMIT),
        name="window",
    )(everyone, *tables)
    terms = terms.reshape(devices, local_rows, 2 * slab)
    arrived = lax.all_to_all(terms, axes, split_axis=0, concat_axis=0, tiled=True)
    factor = 1.0 / math.sqrt(column_count * subgrid_count)
    summed = jnp.sum(arrived.astype(F32), axis=0) * factor
    return summed.reshape(1, local_rows, 2, slab)


def solution(mesh):
    return jax.shard_map(
        body,
        mesh=mesh,
        in_specs=(P("facet", "col", None, None), P("col", None), P("col"), P("col", "facet"), P()),
        out_specs=P("facet", "col", None, None),
        check_vma=False,
    )
```

```python
import functools
import math

import jax
import jax.numpy as jnp
from jax import lax
from jax.experimental import pallas as pl
from jax.experimental.pallas import tpu as pltpu
from jax.sharding import PartitionSpec as P

XC = 64
NPAD = 8192
STEP = 7
ROWS = 8
LANES = 128
CHUNK = 256
HALF = 7
UNROLL = False
VMEM_LIMIT = 24 * 2**20
F32 = jnp.float32
BF16 = jnp.bfloat16
VMEM = pltpu.MemorySpace.VMEM


def wave(number, period, scale):
    quarter = period // 4
    bits = quarter.bit_length() - 1
    turn = (number + quarter // 2) >> bits
    angle = (number - (turn << bits)).astype(F32) * (2.0 * math.pi / period)
    square = angle * angle
    sine = angle * (1.0 + square * (-1 / 6 + square * (1 / 120 + square * (-1 / 5040))))
    cosine = 1.0 + square * (-1 / 2 + square * (1 / 24 + square * (-1 / 720 + square * (1 / 40320))))
    odd = (turn & 1) == 1
    first = jnp.where(odd, sine, cosine)
    second = jnp.where(odd, cosine, sine)
    first = jnp.where(((turn + 1) & 2) == 2, -scale, scale) * first
    second = jnp.where((turn & 2) == 2, -scale, scale) * second
    return first, second


def each(count, step):
    if count == 1:
        step(0)
    else:
        lax.fori_loop(0, count, lambda i, c: (step(i), c)[1], 0)


def iota(shape, axis):
    return lax.broadcasted_iota(jnp.int32, shape, axis)


def ladder(first, step, count):
    real, imag = first
    reals, imags = [real], [imag]
    for _ in range(count - 1):
        real, imag = real * step[0] - imag * step[1], real * step[1] + imag * step[0]
        reals.append(real)
        imags.append(imag)
    return jnp.concatenate(reals, axis=0), jnp.concatenate(imags, axis=0)


def fourier(rows, row_start, lane_numbers, period, scale):
    shape = (ROWS, lane_numbers.shape[1])
    lanes = jnp.broadcast_to(lane_numbers, shape) & (period - 1)
    top = (iota(shape, 0) + row_start) & (period - 1)
    first = wave((top * lanes) & (period - 1), period, scale)
    return ladder(first, wave((ROWS * lanes) & (period - 1), period, 1.0), rows // ROWS)


def block(real, imag, flip):
    low, high = (imag, -imag) if flip else (-imag, imag)
    return jnp.concatenate(
        [jnp.concatenate([real, high], axis=1), jnp.concatenate([low, real], axis=1)], axis=0
    )


def tables_kernel(
    dims, numbers_hbm, screens_ref,
    a_ref, wp_ref, wt_ref, w_ref, wph_ref, ah_ref, gain_ref,
    numbers_ref, small_sem, sem,
):
    facets, height, span, slab, size, owned, chunk = dims
    rows = facets * height
    small = pltpu.make_async_copy(numbers_hbm, numbers_ref, small_sem)
    small.start()

    scale = 1.0 / math.sqrt(size)
    real, imag = fourier(size, 0, iota((1, span), 1), size, scale)
    w_real, w_imag = real.astype(BF16), imag.astype(BF16)
    w_both = jnp.concatenate([w_real, w_imag], axis=1)
    w_ref[...] = w_both
    real, imag = fourier(span, 0, iota((1, size), 1), size, scale)
    wt_ref[...] = block(real.astype(BF16), imag.astype(BF16), False)

    small.wait()
    copies = [
        pltpu.make_async_copy(screens_ref.at[numbers_ref[1 + k]], gain_ref.at[k], sem.at[k])
        for k in range(owned)
    ]
    for copy in copies:
        copy.start()
    column = numbers_ref[0]

    def facet_tables(f):
        lag = STEP * f
        lanes = iota((1, span), 1) - lag
        scale = 1.0 / math.sqrt(slab)
        real, imag = fourier(slab, 0, column + lanes, NPAD, scale / math.sqrt(facets))
        inside = jnp.broadcast_to((lanes >= 0) & (lanes < XC), real.shape)
        zero = jnp.zeros_like(real)
        a_ref[f] = block(
            jnp.where(inside, real, zero).astype(BF16),
            jnp.where(inside, -imag, zero).astype(BF16),
            False,
        )
        real, imag = fourier(span, column - lag, iota((1, slab), 1), NPAD, scale)
        down = iota(real.shape, 0) - lag
        inside = (down >= 0) & (down < XC)
        zero = jnp.zeros_like(real)
        ah_ref[f] = block(
            jnp.where(inside, real, zero).astype(BF16),
            jnp.where(inside, -imag, zero).astype(BF16),
            True,
        )

    if rows == chunk:
        for f in range(facets):
            facet_tables(f)
    else:
        each(facets, facet_tables)

    first = 1 + owned + lax.axis_index("facet") * owned
    scale = 1.0 / math.sqrt(height)
    shift = height.bit_length() - 1

    def row_chunk(k, i):
        fixed = isinstance(i, int)
        base = i * chunk

        def along(start):
            return pl.ds(start, chunk) if fixed else pl.ds(pl.multiple_of(start, chunk), chunk)

        offset = numbers_ref[first + k]
        row = iota((1, chunk), 1) + base
        lag = STEP * (row >> shift)
        low = jnp.broadcast_to((offset - lag) & (NPAD - 1), (ROWS, chunk))
        lanes = jnp.broadcast_to(row & (NPAD - 1), (ROWS, chunk))
        top = (low + iota((ROWS, chunk), 0)) & (NPAD - 1)
        real, imag = ladder(
            wave((top * lanes) & (NPAD - 1), NPAD, scale),
            wave((ROWS * lanes) & (NPAD - 1), NPAD, 1.0),
            span // ROWS,
        )
        u = iota((span, chunk), 0) - lag
        inside = (u >= 0) & (u < XC)
        zero = jnp.zeros_like(real)
        real = jnp.where(inside, real, zero).astype(BF16)
        imag = jnp.where(inside, -imag, zero).astype(BF16)
        both = dot(w_both, block(real, imag, False)).astype(BF16)
        wp_ref[k, :size, along(base)] = both[:, :chunk]
        wp_ref[k, size:, along(base)] = both[:, chunk:]
        reals, imags = [], []
        for f in range(chunk // height):
            lag = STEP * ((base >> shift) + f)
            lanes = iota((1, span), 1) - lag
            real, imag = fourier(height, base + f * height, lanes + offset, NPAD, scale)
            inside = jnp.broadcast_to((lanes >= 0) & (lanes < XC), real.shape)
            zero = jnp.zeros_like(real)
            reals.append(jnp.where(inside, real, zero).astype(BF16))
            imags.append(jnp.where(inside, -imag, zero).astype(BF16))
        both = jnp.concatenate(
            [jnp.concatenate(reals, axis=0), jnp.concatenate(imags, axis=0)], axis=1
        )
        wph_ref[k, along(base), :] = dot(both, wt_ref[...]).astype(BF16)

    for k in range(owned):
        each(rows // chunk, functools.partial(row_chunk, k))
    for copy in copies:
        copy.wait()


def dot(first, second):
    return jnp.dot(first, second, preferred_element_type=F32)


def main_kernel(
    dims, x_ref, a_ref, wp_ref, wt_ref, w_ref, wph_ref, ah_ref, gain_ref, out_ref, spread_ref,
):
    facets, height, span, slab, size, owned, chunk = dims
    rows = facets * height

    def by_facet(value, i, table_ref):
        parts = []
        for f in range(chunk // height):
            own = value[f * height : (f + 1) * height]
            parts.append(dot(own, table_ref[i * (chunk // height) + f]).astype(BF16))
        return parts[0] if len(parts) == 1 else jnp.concatenate(parts, axis=0)

    def along(i):
        base = i * chunk
        return pl.ds(base, chunk) if isinstance(i, int) else pl.ds(pl.multiple_of(base, chunk), chunk)

    def spread(i):
        spread_ref[along(i), :] = by_facet(x_ref[along(i), :], i, a_ref)

    each(rows // chunk, spread)
    inners = []
    for k in range(owned):
        first = dot(wp_ref[k, :size], spread_ref[...])
        second = dot(wp_ref[k, size:], spread_ref[...])
        half = jnp.concatenate(
            [first[:, :span] - second[:, span:], first[:, span:] + second[:, :span]], axis=1
        ).astype(BF16)
        grid = dot(half, wt_ref[...])
        real, imag = grid[:, :size], grid[:, size:]
        gain_real, gain_imag = gain_ref[k, 0], gain_ref[k, 1]
        seen_real = (real * gain_real - imag * gain_imag).astype(BF16)
        seen_imag = (real * gain_imag + imag * gain_real).astype(BF16)
        first = dot(seen_real, w_ref[...])
        second = dot(seen_imag, w_ref[...])
        inners.append(
            jnp.concatenate(
                [first[:, :span] + second[:, span:], second[:, :span] - first[:, span:]], axis=1
            ).astype(BF16)
        )

    def back(i):
        own = 0.0
        for k in range(owned):
            first = dot(wph_ref[k, along(i), :size], inners[k])
            second = dot(wph_ref[k, along(i), size:], inners[k])
            own += jnp.concatenate(
                [first[:, :span] + second[:, span:], first[:, span:] - second[:, :span]], axis=1
            )
        out_ref[along(i), :] = by_facet(own.astype(BF16), i, ah_ref)

    each(rows // chunk, back)


def pair_send_kernel(facets_ref, sub_hbm, col_ref, pick_ref, out_ref, mine_ref, sub_ref, sem):
    copies = [
        pltpu.make_async_copy(facets_ref, mine_ref, sem.at[0]),
        pltpu.make_async_copy(sub_hbm, sub_ref, sem.at[1]),
    ]
    for copy in copies:
        copy.start()
    for copy in copies:
        copy.wait()
    numbers = (col_ref[0], sub_ref[0, lax.axis_index("facet")], pick_ref[0, 0])
    lane = iota((facets_ref.shape[1], LANES), 1)
    told = jnp.zeros(lane.shape, jnp.int32)
    for i, number in enumerate(numbers):
        told = jnp.where(lane == i, number >> HALF, told)
        told = jnp.where(lane == i + len(numbers), number & ((1 << HALF) - 1), told)
    mine = jnp.concatenate(
        [mine_ref[0, :, 0, :], mine_ref[0, :, 1, :], told.astype(F32).astype(BF16)], axis=1
    )
    out_ref[...] = jnp.broadcast_to(mine[None], out_ref.shape)


def fine_dot(first, second):
    parts = []
    for value in (first, second):
        high = value.astype(BF16)
        parts.append((high, (value - high.astype(F32)).astype(BF16)))
    (a, a_rest), (b, b_rest) = parts
    return dot(a, b) + (dot(a, b_rest) + dot(a_rest, b))


def pair_tables_kernel(
    dims, screens_hbm, a_ref, wp_ref, wt_ref, low_ref, wa_ref, screens_ref, sem
):
    facets, height, span, slab, size, columns, local = dims
    rows = facets * height
    copy = pltpu.make_async_copy(screens_hbm, screens_ref, sem)
    copy.start()
    scale = 1.0 / math.sqrt(size)
    w_both = jnp.concatenate(fourier(size, 0, iota((1, span), 1), size, scale), axis=1)
    w_turned = block(*fourier(span, 0, iota((1, size), 1), size, scale), False)
    wt_ref[...] = w_turned.astype(BF16)

    def keep(number, real, imag):
        inside = jnp.broadcast_to((number >= 0) & (number < XC), real.shape)
        zero = jnp.zeros_like(real)
        return jnp.where(inside, real, zero), jnp.where(inside, -imag, zero)

    facet = lax.axis_index("facet")
    lag = STEP * facet
    scale = 1.0 / math.sqrt(slab)
    for f in range(facets):
        lanes = iota((1, span), 1) - STEP * f
        real, imag = keep(lanes, *fourier(slab, 0, lanes, NPAD, scale / math.sqrt(facets)))
        a_ref[f] = block(real.astype(BF16), imag.astype(BF16), False)
    real, imag = fourier(span, -lag, iota((1, slab), 1), NPAD, scale)
    both = fine_dot(w_both, block(*keep(iota(real.shape, 0) - lag, real, imag), False))
    wa_ref[:, :slab] = both[:, :slab].astype(BF16)
    wa_ref[:, slab:] = (-both[:, slab:]).astype(BF16)

    scale = 1.0 / math.sqrt(height)
    row = iota((1, rows), 1)
    behind = STEP * (row >> (height.bit_length() - 1))
    lanes = jnp.broadcast_to(row & (NPAD - 1), (ROWS, rows))
    top = (jnp.broadcast_to(-behind, (ROWS, rows)) + iota((ROWS, rows), 0)) & (NPAD - 1)
    real, imag = ladder(
        wave((top * lanes) & (NPAD - 1), NPAD, scale),
        wave((ROWS * lanes) & (NPAD - 1), NPAD, 1.0),
        span // ROWS,
    )
    both = fine_dot(w_both, block(*keep(iota(real.shape, 0) - behind, real, imag), False)).astype(BF16)
    wp_ref[:size] = both[:, :rows]
    wp_ref[size:] = both[:, rows:]

    pair_rows = 2 * local
    base = facet * height + (lax.axis_index("col") >> 1) * pair_rows
    lanes = iota((1, span), 1) - lag
    real, imag = keep(lanes, *fourier(pair_rows, base, lanes, NPAD, scale))
    both = fine_dot(jnp.concatenate([real, imag], axis=1), w_turned).astype(BF16)
    low_ref[:pair_rows] = both[:, :size]
    low_ref[pair_rows:] = both[:, size:]
    copy.wait()


def dot_nt(first, second):
    return lax.dot_general(first, second, (((1,), (1,)), ((), ())), preferred_element_type=F32)


def pair_kernel(
    dims, x_ref, a_ref, wp_ref, wt_ref, low_ref, wa_ref, screens_ref, mine_ref, other_ref,
    told_ref, numbers_ref, spread_ref, down_ref, half_ref, lifted_ref, seen_ref, gathered_ref, phase_ref, sem,
):
    facets, height, span, slab, size, columns, local = dims
    rows = facets * height
    subgrids = facets
    pair_rows = 2 * local
    mine_columns = columns // 2
    core = lax.axis_index("col") & 1
    base = lax.axis_index("facet") * height + (lax.axis_index("col") >> 1) * pair_rows

    lane, line = iota((ROWS, LANES), 1), iota((ROWS, LANES), 0)
    weights = jnp.where(lane == line, 1 << HALF, jnp.where(lane == line + 3, 1, 0))
    weights = jnp.where(line < 3, weights, 0).astype(F32).astype(BF16)
    told = dot_nt(weights, x_ref[:, 2 * slab :])
    told_ref[...] = told.astype(jnp.int32)
    copy = pltpu.make_async_copy(told_ref, numbers_ref, sem)
    copy.start()
    copy.wait()

    def number(kind, facet, column):
        return numbers_ref[kind, (facet * columns + column) * local]

    def times(a, b):
        return a[0] * b[0] - a[1] * b[1], a[0] * b[1] + a[1] * b[0]

    def phases(offset, where):
        real, imag = wave((where * offset) & (NPAD - 1), NPAD, 1.0)
        return real, -imag

    for i in range(mine_columns):
        column = 2 * i + core
        ahead = phases(number(0, 0, column), iota((ROWS, slab), 1))
        phase_ref[2 * i * ROWS : (2 * i + 1) * ROWS, :] = ahead[0]
        phase_ref[(2 * i + 1) * ROWS : (2 * i + 2) * ROWS, :] = ahead[1]
        line = iota((ROWS, rows), 0)
        offset_rows = jnp.zeros((ROWS, rows), jnp.int32)
        for s in range(subgrids):
            offset_rows = jnp.where(line == s, number(1, s, column), offset_rows)
        row_phase = phases(offset_rows, iota((ROWS, rows), 1))
        for h in (0, 1):
            down_ref[i, h, :, :ROWS] = row_phase[h].T
        own = x_ref[:, : 2 * slab].astype(F32)
        real, imag = times(
            (own[:, :slab], own[:, slab:]),
            [jnp.broadcast_to(p[:1], (rows, slab)) for p in ahead],
        )
        turned = jnp.concatenate([real.astype(BF16), imag.astype(BF16)], axis=1)
        for f in range(facets):
            part = slice(f * height, (f + 1) * height)
            spread_ref[i, part, :] = dot(turned[part], a_ref[f])

    def one_column(i):
        for s in range(subgrids):
            down = [jnp.broadcast_to(down_ref[i, h, :, s : s + 1], (rows, span)) for h in (0, 1)]
            real, imag = times((spread_ref[i, :, :span], spread_ref[i, :, span:]), down)
            lifted_ref[s, :, :span] = real.astype(BF16)
            lifted_ref[s, :, span:] = imag.astype(BF16)
        for s in range(subgrids):
            lifted = lifted_ref[s]
            first = dot(wp_ref[:size], lifted)
            second = dot(wp_ref[size:], lifted)
            half_ref[s * size : (s + 1) * size, :span] = (first[:, :span] - second[:, span:]).astype(BF16)
            half_ref[s * size : (s + 1) * size, span:] = (first[:, span:] + second[:, :span]).astype(BF16)
        half = half_ref[...]
        all_real, all_imag = dot(half, wt_ref[:, :size]), dot(half, wt_ref[:, size:])
        for s in range(subgrids):
            part = slice(s * size, (s + 1) * size)
            real, imag = all_real[part], all_imag[part]
            pick = number(2, s, 2 * i + core)
            gain_real, gain_imag = screens_ref[pick, 0], screens_ref[pick, 1]
            seen_ref[s, 0] = (real * gain_real - imag * gain_imag).astype(BF16)
            seen_ref[s, 1] = (real * gain_imag + imag * gain_real).astype(BF16)
        sums = None
        for s in range(subgrids):
            first = dot(low_ref[...], seen_ref[s, 0])
            second = dot(low_ref[...], seen_ref[s, 1])
            real = first[:pair_rows] + second[pair_rows:]
            imag = second[:pair_rows] - first[pair_rows:]
            back = [
                jnp.broadcast_to(down_ref[i, h, pl.ds(base, pair_rows), s : s + 1], (pair_rows, size))
                for h in (0, 1)
            ]
            term = times((real, imag), (back[0], -back[1]))
            sums = term if sums is None else (sums[0] + term[0], sums[1] + term[1])
        start = pl.multiple_of(i * pair_rows, pair_rows)
        gathered_ref[pl.ds(start, pair_rows), :size] = sums[0].astype(BF16)
        gathered_ref[pl.ds(start, pair_rows), size:] = sums[1].astype(BF16)

    lax.fori_loop(0, mine_columns, lambda i, c: (one_column(i), c)[1], 0)

    first = dot(gathered_ref[:, :size], wa_ref[...])
    second = dot(gathered_ref[:, size:], wa_ref[...])
    real = first[:, :slab] - second[:, slab:]
    imag = first[:, slab:] + second[:, :slab]
    total = None
    for i in range(mine_columns):
        part = slice(i * pair_rows, (i + 1) * pair_rows)
        back_real = jnp.broadcast_to(phase_ref[i * 2 * ROWS : i * 2 * ROWS + 1], (pair_rows, slab))
        back_imag = jnp.broadcast_to(
            phase_ref[i * 2 * ROWS + ROWS : i * 2 * ROWS + ROWS + 1], (pair_rows, slab)
        )
        term = times((real[part], imag[part]), (back_real, -back_imag))
        total = term if total is None else (total[0] + term[0], total[1] + term[1])
    both = jnp.concatenate(total, axis=1)
    mine_ref[...] = jnp.where(core == 0, both[:local], both[local:])
    other_ref[...] = jnp.where(core == 0, both[local:], both[:local])


def pair_body(facets, sub_offsets, col_offsets, screen_index, screens):
    facet_count = lax.axis_size("facet")
    column_count = lax.axis_size("col")
    devices = facet_count * column_count
    local_rows, slab = facets.shape[1], facets.shape[3]
    height = local_rows * column_count
    rows = facet_count * height
    subgrid_count = sub_offsets.shape[1]
    size = screens.shape[2]
    span = -(-(XC + STEP * (facet_count - 1)) // LANES) * LANES
    dims = (facet_count, height, span, slab, size, column_count, local_rows)
    any_space = pl.BlockSpec(memory_space=pl.ANY)
    smem = pl.BlockSpec(memory_space=pltpu.MemorySpace.SMEM)
    width = 2 * slab + LANES

    outgoing = pl.pallas_call(
        pair_send_kernel,
        out_shape=jax.ShapeDtypeStruct((devices, local_rows, width), BF16),
        in_specs=[any_space, any_space, smem, smem],
        out_specs=pl.BlockSpec(memory_space=VMEM),
        scratch_shapes=[
            pltpu.VMEM(facets.shape, BF16),
            pltpu.SMEM(sub_offsets.shape, jnp.int32),
            pltpu.SemaphoreType.DMA((2,)),
        ],
        compiler_params=pltpu.CompilerParams(vmem_limit_bytes=VMEM_LIMIT),
        name="send",
    )(in_hbm(facets), in_hbm(sub_offsets), col_offsets, screen_index)
    everyone = lax.all_to_all(
        outgoing, ("facet", "col"), split_axis=0, concat_axis=0, tiled=True
    ).reshape(rows, width)
    table_shapes = [
        ((facet_count, 2 * span, 2 * slab), BF16),
        ((2 * size, rows), BF16),
        ((2 * span, 2 * size), BF16),
        ((4 * local_rows, size), BF16),
        ((size, 2 * slab), BF16),
        (screens.shape, F32),
    ]
    table_bytes = sum(math.prod(s) * jnp.dtype(t).itemsize for s, t in table_shapes)
    tables = pl.pallas_call(
        functools.partial(pair_tables_kernel, dims),
        out_shape=[jax.ShapeDtypeStruct(s, t) for s, t in table_shapes],
        in_specs=[any_space],
        out_specs=whole(len(table_shapes)),
        scratch_shapes=[pltpu.SemaphoreType.DMA],
        compiler_params=pltpu.CompilerParams(vmem_limit_bytes=VMEM_LIMIT),
        cost_estimate=pl.CostEstimate(
            flops=100 * table_bytes, bytes_accessed=2 * table_bytes, transcendentals=0
        ),
        name="tables",
    )(in_hbm(screens))
    mine, other = pl.pallas_call(
        functools.partial(pair_kernel, dims),
        out_shape=[jax.ShapeDtypeStruct((local_rows, 2 * slab), F32)] * 2,
        in_specs=whole(1 + len(tables)),
        out_specs=whole(2),
        scratch_shapes=[
            pltpu.VMEM((ROWS, rows), jnp.int32),
            pltpu.SMEM((ROWS, rows), jnp.int32),
            pltpu.VMEM((column_count // 2, rows, 2 * span), F32),
            pltpu.VMEM((column_count // 2, 2, rows, LANES), F32),
            pltpu.VMEM((subgrid_count * size, 2 * span), BF16),
            pltpu.VMEM((subgrid_count, rows, 2 * span), BF16),
            pltpu.VMEM((subgrid_count, 2, size, size), BF16),
            pltpu.VMEM((column_count * local_rows, 2 * size), BF16),
            pltpu.VMEM((column_count * ROWS, slab), F32),
            pltpu.SemaphoreType.DMA,
        ],
        compiler_params=pltpu.CompilerParams(vmem_limit_bytes=VMEM_LIMIT),
        name="window",
    )(everyone, *tables)
    swap = [(i, i ^ 1) for i in range(column_count)]
    summed = mine + lax.ppermute(other, "col", swap)
    return (summed / math.sqrt(column_count * subgrid_count)).reshape(1, local_rows, 2, slab)


def send_kernel(facets_ref, out_ref, mine_ref, sem):
    copy = pltpu.make_async_copy(facets_ref, mine_ref, sem)
    copy.start()
    copy.wait()
    mine = jnp.concatenate([mine_ref[0, :, 0, :], mine_ref[0, :, 1, :]], axis=1)
    out_ref[...] = jnp.broadcast_to(mine[None], out_ref.shape)


def in_hbm(array):
    return pltpu.with_memory_space_constraint(array, pltpu.MemorySpace.HBM)


def whole(count):
    return [pl.BlockSpec(memory_space=VMEM)] * count


def spread_body(facets, sub_offsets, col_offsets, screen_index, screens):
    axes = ("facet", "col")
    facet_count = lax.axis_size("facet")
    column_count = lax.axis_size("col")
    devices = facet_count * column_count
    local_rows, slab = facets.shape[1], facets.shape[3]
    height = local_rows * column_count
    rows = facet_count * height
    subgrid_count = sub_offsets.shape[1]
    owned = subgrid_count // facet_count
    size = screens.shape[2]
    span = -(-(XC + STEP * (facet_count - 1)) // LANES) * LANES
    chunk = max(height, min(rows, CHUNK))
    dims = (facet_count, height, span, slab, size, owned, chunk)

    outgoing = pl.pallas_call(
        send_kernel,
        out_shape=jax.ShapeDtypeStruct((devices, local_rows, 2 * slab), BF16),
        in_specs=[pl.BlockSpec(memory_space=pl.ANY)],
        out_specs=pl.BlockSpec(memory_space=VMEM),
        scratch_shapes=[pltpu.VMEM(facets.shape, BF16), pltpu.SemaphoreType.DMA],
        compiler_params=pltpu.CompilerParams(vmem_limit_bytes=VMEM_LIMIT),
        name="send",
    )(in_hbm(facets))
    everyone = lax.all_to_all(outgoing, axes, split_axis=0, concat_axis=0, tiled=True)
    everyone = everyone.reshape(rows, 2 * slab)
    numbers = jnp.concatenate([col_offsets, screen_index[0], sub_offsets[0]])
    table_shapes = [
        ((facet_count, 2 * slab, 2 * span), BF16),
        ((owned, 2 * size, rows), BF16),
        ((2 * span, 2 * size), BF16),
        ((size, 2 * span), BF16),
        ((owned, rows, 2 * size), BF16),
        ((facet_count, 2 * span, 2 * slab), BF16),
        ((owned, 2, size, size), F32),
    ]
    table_bytes = sum(math.prod(s) * jnp.dtype(t).itemsize for s, t in table_shapes)
    tables = pl.pallas_call(
        functools.partial(tables_kernel, dims),
        out_shape=[jax.ShapeDtypeStruct(s, t) for s, t in table_shapes],
        in_specs=[pl.BlockSpec(memory_space=pl.ANY)] * 2,
        out_specs=whole(len(table_shapes)),
        scratch_shapes=[
            pltpu.SMEM(numbers.shape, jnp.int32),
            pltpu.SemaphoreType.DMA,
            pltpu.SemaphoreType.DMA((owned,)),
        ],
        compiler_params=pltpu.CompilerParams(vmem_limit_bytes=VMEM_LIMIT),
        cost_estimate=pl.CostEstimate(
            flops=100 * table_bytes, bytes_accessed=2 * table_bytes, transcendentals=0
        ),
        name="tables",
    )(numbers, in_hbm(screens))
    terms = pl.pallas_call(
        functools.partial(main_kernel, dims),
        out_shape=jax.ShapeDtypeStruct((rows, 2 * slab), BF16),
        in_specs=whole(1 + len(tables)),
        out_specs=pl.BlockSpec(memory_space=VMEM),
        scratch_shapes=[pltpu.VMEM((rows, 2 * span), BF16)],
        compiler_params=pltpu.CompilerParams(vmem_limit_bytes=VMEM_LIMIT),
        name="window",
    )(everyone, *tables)
    terms = terms.reshape(devices, local_rows, 2 * slab)
    arrived = lax.all_to_all(terms, axes, split_axis=0, concat_axis=0, tiled=True)
    factor = 1.0 / math.sqrt(column_count * subgrid_count)
    summed = jnp.sum(arrived.astype(F32), axis=0) * factor
    return summed.reshape(1, local_rows, 2, slab)


def body(facets, sub_offsets, col_offsets, screen_index, screens):
    columns, subgrids = lax.axis_size("col"), sub_offsets.shape[1]
    alone = columns % 2 == 0 and subgrids == lax.axis_size("facet") and columns * subgrids <= 32
    run = pair_body if alone else spread_body
    return run(facets, sub_offsets, col_offsets, screen_index, screens)


def solution(mesh):
    return jax.shard_map(
        body,
        mesh=mesh,
        in_specs=(P("facet", "col", None, None), P("col", None), P("col"), P("col", "facet"), P()),
        out_specs=P("facet", "col", None, None),
        check_vma=False,
    )
```

```python
import functools
import math

import jax
import jax.numpy as jnp
from jax import lax
from jax.experimental import pallas as pl
from jax.experimental.pallas import tpu as pltpu
from jax.sharding import PartitionSpec as P

XC = 64
NPAD = 8192
STEP = 7
ROWS = 8
LANES = 128
CHUNK = 256
HALF = 7
UNROLL = False
VMEM_LIMIT = 24 * 2**20
F32 = jnp.float32
BF16 = jnp.bfloat16
VMEM = pltpu.MemorySpace.VMEM


def wave(number, period, scale):
    quarter = period // 4
    bits = quarter.bit_length() - 1
    turn = (number + quarter // 2) >> bits
    angle = (number - (turn << bits)).astype(F32) * (2.0 * math.pi / period)
    square = angle * angle
    sine = angle * (1.0 + square * (-1 / 6 + square * (1 / 120 + square * (-1 / 5040))))
    cosine = 1.0 + square * (-1 / 2 + square * (1 / 24 + square * (-1 / 720 + square * (1 / 40320))))
    odd = (turn & 1) == 1
    first = jnp.where(odd, sine, cosine)
    second = jnp.where(odd, cosine, sine)
    first = jnp.where(((turn + 1) & 2) == 2, -scale, scale) * first
    second = jnp.where((turn & 2) == 2, -scale, scale) * second
    return first, second


def each(count, step):
    if count == 1:
        step(0)
    else:
        lax.fori_loop(0, count, lambda i, c: (step(i), c)[1], 0)


def iota(shape, axis):
    return lax.broadcasted_iota(jnp.int32, shape, axis)


def ladder(first, step, count):
    real, imag = first
    reals, imags = [real], [imag]
    for _ in range(count - 1):
        real, imag = real * step[0] - imag * step[1], real * step[1] + imag * step[0]
        reals.append(real)
        imags.append(imag)
    return jnp.concatenate(reals, axis=0), jnp.concatenate(imags, axis=0)


def fourier(rows, row_start, lane_numbers, period, scale):
    shape = (ROWS, lane_numbers.shape[1])
    lanes = jnp.broadcast_to(lane_numbers, shape) & (period - 1)
    top = (iota(shape, 0) + row_start) & (period - 1)
    first = wave((top * lanes) & (period - 1), period, scale)
    return ladder(first, wave((ROWS * lanes) & (period - 1), period, 1.0), rows // ROWS)


def block(real, imag, flip):
    low, high = (imag, -imag) if flip else (-imag, imag)
    return jnp.concatenate(
        [jnp.concatenate([real, high], axis=1), jnp.concatenate([low, real], axis=1)], axis=0
    )


def tables_kernel(
    dims, numbers_hbm, screens_ref,
    a_ref, wp_ref, wt_ref, w_ref, wph_ref, ah_ref, gain_ref,
    numbers_ref, small_sem, sem,
):
    facets, height, span, slab, size, owned, chunk = dims
    rows = facets * height
    small = pltpu.make_async_copy(numbers_hbm, numbers_ref, small_sem)
    small.start()

    scale = 1.0 / math.sqrt(size)
    real, imag = fourier(size, 0, iota((1, span), 1), size, scale)
    w_real, w_imag = real.astype(BF16), imag.astype(BF16)
    w_both = jnp.concatenate([w_real, w_imag], axis=1)
    w_ref[...] = w_both
    real, imag = fourier(span, 0, iota((1, size), 1), size, scale)
    wt_ref[...] = block(real.astype(BF16), imag.astype(BF16), False)

    small.wait()
    copies = [
        pltpu.make_async_copy(screens_ref.at[numbers_ref[1 + k]], gain_ref.at[k], sem.at[k])
        for k in range(owned)
    ]
    for copy in copies:
        copy.start()
    column = numbers_ref[0]

    def facet_tables(f):
        lag = STEP * f
        lanes = iota((1, span), 1) - lag
        scale = 1.0 / math.sqrt(slab)
        real, imag = fourier(slab, 0, column + lanes, NPAD, scale / math.sqrt(facets))
        inside = jnp.broadcast_to((lanes >= 0) & (lanes < XC), real.shape)
        zero = jnp.zeros_like(real)
        a_ref[f] = block(
            jnp.where(inside, real, zero).astype(BF16),
            jnp.where(inside, -imag, zero).astype(BF16),
            False,
        )
        real, imag = fourier(span, column - lag, iota((1, slab), 1), NPAD, scale)
        down = iota(real.shape, 0) - lag
        inside = (down >= 0) & (down < XC)
        zero = jnp.zeros_like(real)
        ah_ref[f] = block(
            jnp.where(inside, real, zero).astype(BF16),
            jnp.where(inside, -imag, zero).astype(BF16),
            True,
        )

    if rows == chunk:
        for f in range(facets):
            facet_tables(f)
    else:
        each(facets, facet_tables)

    first = 1 + owned + lax.axis_index("facet") * owned
    scale = 1.0 / math.sqrt(height)
    shift = height.bit_length() - 1

    def row_chunk(k, i):
        fixed = isinstance(i, int)
        base = i * chunk

        def along(start):
            return pl.ds(start, chunk) if fixed else pl.ds(pl.multiple_of(start, chunk), chunk)

        offset = numbers_ref[first + k]
        row = iota((1, chunk), 1) + base
        lag = STEP * (row >> shift)
        low = jnp.broadcast_to((offset - lag) & (NPAD - 1), (ROWS, chunk))
        lanes = jnp.broadcast_to(row & (NPAD - 1), (ROWS, chunk))
        top = (low + iota((ROWS, chunk), 0)) & (NPAD - 1)
        real, imag = ladder(
            wave((top * lanes) & (NPAD - 1), NPAD, scale),
            wave((ROWS * lanes) & (NPAD - 1), NPAD, 1.0),
            span // ROWS,
        )
        u = iota((span, chunk), 0) - lag
        inside = (u >= 0) & (u < XC)
        zero = jnp.zeros_like(real)
        real = jnp.where(inside, real, zero).astype(BF16)
        imag = jnp.where(inside, -imag, zero).astype(BF16)
        both = dot(w_both, block(real, imag, False)).astype(BF16)
        wp_ref[k, :size, along(base)] = both[:, :chunk]
        wp_ref[k, size:, along(base)] = both[:, chunk:]
        reals, imags = [], []
        for f in range(chunk // height):
            lag = STEP * ((base >> shift) + f)
            lanes = iota((1, span), 1) - lag
            real, imag = fourier(height, base + f * height, lanes + offset, NPAD, scale)
            inside = jnp.broadcast_to((lanes >= 0) & (lanes < XC), real.shape)
            zero = jnp.zeros_like(real)
            reals.append(jnp.where(inside, real, zero).astype(BF16))
            imags.append(jnp.where(inside, -imag, zero).astype(BF16))
        both = jnp.concatenate(
            [jnp.concatenate(reals, axis=0), jnp.concatenate(imags, axis=0)], axis=1
        )
        wph_ref[k, along(base), :] = dot(both, wt_ref[...]).astype(BF16)

    for k in range(owned):
        each(rows // chunk, functools.partial(row_chunk, k))
    for copy in copies:
        copy.wait()


def dot(first, second):
    return jnp.dot(first, second, preferred_element_type=F32)


def main_kernel(
    dims, x_ref, a_ref, wp_ref, wt_ref, w_ref, wph_ref, ah_ref, gain_ref, out_ref, spread_ref,
):
    facets, height, span, slab, size, owned, chunk = dims
    rows = facets * height

    def by_facet(value, i, table_ref):
        parts = []
        for f in range(chunk // height):
            own = value[f * height : (f + 1) * height]
            parts.append(dot(own, table_ref[i * (chunk // height) + f]).astype(BF16))
        return parts[0] if len(parts) == 1 else jnp.concatenate(parts, axis=0)

    def along(i):
        base = i * chunk
        return pl.ds(base, chunk) if isinstance(i, int) else pl.ds(pl.multiple_of(base, chunk), chunk)

    def spread(i):
        spread_ref[along(i), :] = by_facet(x_ref[along(i), :], i, a_ref)

    each(rows // chunk, spread)
    inners = []
    for k in range(owned):
        first = dot(wp_ref[k, :size], spread_ref[...])
        second = dot(wp_ref[k, size:], spread_ref[...])
        half = jnp.concatenate(
            [first[:, :span] - second[:, span:], first[:, span:] + second[:, :span]], axis=1
        ).astype(BF16)
        grid = dot(half, wt_ref[...])
        real, imag = grid[:, :size], grid[:, size:]
        gain_real, gain_imag = gain_ref[k, 0], gain_ref[k, 1]
        seen_real = (real * gain_real - imag * gain_imag).astype(BF16)
        seen_imag = (real * gain_imag + imag * gain_real).astype(BF16)
        first = dot(seen_real, w_ref[...])
        second = dot(seen_imag, w_ref[...])
        inners.append(
            jnp.concatenate(
                [first[:, :span] + second[:, span:], second[:, :span] - first[:, span:]], axis=1
            ).astype(BF16)
        )

    def back(i):
        own = 0.0
        for k in range(owned):
            first = dot(wph_ref[k, along(i), :size], inners[k])
            second = dot(wph_ref[k, along(i), size:], inners[k])
            own += jnp.concatenate(
                [first[:, :span] + second[:, span:], first[:, span:] - second[:, :span]], axis=1
            )
        out_ref[along(i), :] = by_facet(own.astype(BF16), i, ah_ref)

    each(rows // chunk, back)


def pair_send_kernel(facets_ref, sub_hbm, col_ref, pick_ref, out_ref, mine_ref, sub_ref, sem):
    copies = [
        pltpu.make_async_copy(facets_ref, mine_ref, sem.at[0]),
        pltpu.make_async_copy(sub_hbm, sub_ref, sem.at[1]),
    ]
    for copy in copies:
        copy.start()
    for copy in copies:
        copy.wait()
    numbers = (col_ref[0], sub_ref[0, lax.axis_index("facet")], pick_ref[0, 0])
    lane = iota((facets_ref.shape[1], LANES), 1)
    told = jnp.zeros(lane.shape, jnp.int32)
    for i, number in enumerate(numbers):
        told = jnp.where(lane == i, number >> HALF, told)
        told = jnp.where(lane == i + len(numbers), number & ((1 << HALF) - 1), told)
    mine = jnp.concatenate(
        [mine_ref[0, :, 0, :], mine_ref[0, :, 1, :], told.astype(F32).astype(BF16)], axis=1
    )
    out_ref[...] = jnp.broadcast_to(mine[None], out_ref.shape)


def fine_dot(first, second):
    parts = []
    for value in (first, second):
        high = value.astype(BF16)
        parts.append((high, (value - high.astype(F32)).astype(BF16)))
    (a, a_rest), (b, b_rest) = parts
    return dot(a, b) + (dot(a, b_rest) + dot(a_rest, b))


def pair_tables_kernel(
    dims, screens_hbm, a_ref, wp_ref, wt_ref, low_ref, wa_ref, screens_ref, sem
):
    facets, height, span, slab, size, columns, local = dims
    rows = facets * height
    copy = pltpu.make_async_copy(screens_hbm, screens_ref, sem)
    copy.start()
    scale = 1.0 / math.sqrt(size)
    w_both = jnp.concatenate(fourier(size, 0, iota((1, span), 1), size, scale), axis=1)
    w_turned = block(*fourier(span, 0, iota((1, size), 1), size, scale), False)
    wt_ref[...] = w_turned.astype(BF16)

    def keep(number, real, imag):
        inside = jnp.broadcast_to((number >= 0) & (number < XC), real.shape)
        zero = jnp.zeros_like(real)
        return jnp.where(inside, real, zero), jnp.where(inside, -imag, zero)

    facet = lax.axis_index("facet")
    lag = STEP * facet
    scale = 1.0 / math.sqrt(slab)
    for f in range(facets):
        lanes = iota((1, span), 1) - STEP * f
        real, imag = keep(lanes, *fourier(slab, 0, lanes, NPAD, scale / math.sqrt(facets)))
        a_ref[f] = block(real.astype(BF16), imag.astype(BF16), False)
    real, imag = fourier(span, -lag, iota((1, slab), 1), NPAD, scale)
    both = fine_dot(w_both, block(*keep(iota(real.shape, 0) - lag, real, imag), False))
    wa_ref[:, :slab] = both[:, :slab].astype(BF16)
    wa_ref[:, slab:] = (-both[:, slab:]).astype(BF16)

    scale = 1.0 / math.sqrt(height)
    row = iota((1, rows), 1)
    behind = STEP * (row >> (height.bit_length() - 1))
    lanes = jnp.broadcast_to(row & (NPAD - 1), (ROWS, rows))
    top = (jnp.broadcast_to(-behind, (ROWS, rows)) + iota((ROWS, rows), 0)) & (NPAD - 1)
    real, imag = ladder(
        wave((top * lanes) & (NPAD - 1), NPAD, scale),
        wave((ROWS * lanes) & (NPAD - 1), NPAD, 1.0),
        span // ROWS,
    )
    both = fine_dot(w_both, block(*keep(iota(real.shape, 0) - behind, real, imag), False)).astype(BF16)
    wp_ref[:size] = both[:, :rows]
    wp_ref[size:] = both[:, rows:]

    pair_rows = 2 * local
    base = facet * height + (lax.axis_index("col") >> 1) * pair_rows
    lanes = iota((1, span), 1) - lag
    real, imag = keep(lanes, *fourier(pair_rows, base, lanes, NPAD, scale))
    both = fine_dot(jnp.concatenate([real, imag], axis=1), w_turned).astype(BF16)
    low_ref[:pair_rows] = both[:, :size]
    low_ref[pair_rows:] = both[:, size:]
    copy.wait()


def dot_nt(first, second):
    return lax.dot_general(first, second, (((1,), (1,)), ((), ())), preferred_element_type=F32)


def pair_kernel(
    dims, x_ref, a_ref, wp_ref, wt_ref, low_ref, wa_ref, screens_ref, mine_ref, other_ref,
    told_ref, numbers_ref, spread_ref, down_ref, half_ref, lifted_ref, seen_ref, gathered_ref, phase_ref, sem,
):
    facets, height, span, slab, size, columns, local = dims
    rows = facets * height
    subgrids = facets
    pair_rows = 2 * local
    mine_columns = columns // 2
    core = lax.axis_index("col") & 1
    base = lax.axis_index("facet") * height + (lax.axis_index("col") >> 1) * pair_rows

    lane, line = iota((ROWS, LANES), 1), iota((ROWS, LANES), 0)
    weights = jnp.where(lane == line, 1 << HALF, jnp.where(lane == line + 3, 1, 0))
    weights = jnp.where(line < 3, weights, 0).astype(F32).astype(BF16)
    told = dot_nt(weights, x_ref[:, 2 * slab :])
    told_ref[...] = told.astype(jnp.int32)
    copy = pltpu.make_async_copy(told_ref, numbers_ref, sem)
    copy.start()
    copy.wait()

    def number(kind, facet, column):
        return numbers_ref[kind, (facet * columns + column) * local]

    def times(a, b):
        return a[0] * b[0] - a[1] * b[1], a[0] * b[1] + a[1] * b[0]

    def phases(offset, where):
        real, imag = wave((where * offset) & (NPAD - 1), NPAD, 1.0)
        return real, -imag

    for i in range(mine_columns):
        column = 2 * i + core
        ahead = phases(number(0, 0, column), iota((ROWS, slab), 1))
        phase_ref[2 * i * ROWS : (2 * i + 1) * ROWS, :] = ahead[0]
        phase_ref[(2 * i + 1) * ROWS : (2 * i + 2) * ROWS, :] = ahead[1]
        line = iota((ROWS, rows), 0)
        offset_rows = jnp.zeros((ROWS, rows), jnp.int32)
        for s in range(subgrids):
            offset_rows = jnp.where(line == s, number(1, s, column), offset_rows)
        row_phase = phases(offset_rows, iota((ROWS, rows), 1))
        for h in (0, 1):
            down_ref[i, h, :, :ROWS] = row_phase[h].T
        own = x_ref[:, : 2 * slab].astype(F32)
        real, imag = times(
            (own[:, :slab], own[:, slab:]),
            [jnp.broadcast_to(p[:1], (rows, slab)) for p in ahead],
        )
        turned = jnp.concatenate([real.astype(BF16), imag.astype(BF16)], axis=1)
        for f in range(facets):
            part = slice(f * height, (f + 1) * height)
            spread_ref[i, part, :] = dot(turned[part], a_ref[f])

    def lift(i, slot):
        for s in range(subgrids):
            down = [jnp.broadcast_to(down_ref[i, h, :, s : s + 1], (rows, span)) for h in (0, 1)]
            real, imag = times((spread_ref[i, :, :span], spread_ref[i, :, span:]), down)
            lifted_ref[slot, s, :, :span] = real.astype(BF16)
            lifted_ref[slot, s, :, span:] = imag.astype(BF16)

    def one_column(i, slot, following):
        for s in range(subgrids):
            lifted = lifted_ref[slot, s]
            first = dot(wp_ref[:size], lifted)
            second = dot(wp_ref[size:], lifted)
            part = slice(s * size, (s + 1) * size)
            half_ref[slot, part, :span] = (first[:, :span] - second[:, span:]).astype(BF16)
            half_ref[slot, part, span:] = (first[:, span:] + second[:, :span]).astype(BF16)
        if following is not None:
            lift(following, 1 - slot)
        half = half_ref[slot]
        all_real, all_imag = dot(half, wt_ref[:, :size]), dot(half, wt_ref[:, size:])
        for s in range(subgrids):
            part = slice(s * size, (s + 1) * size)
            real, imag = all_real[part], all_imag[part]
            pick = number(2, s, 2 * i + core)
            gain_real, gain_imag = screens_ref[pick, 0], screens_ref[pick, 1]
            seen_ref[slot, s, 0] = (real * gain_real - imag * gain_imag).astype(BF16)
            seen_ref[slot, s, 1] = (real * gain_imag + imag * gain_real).astype(BF16)
        sums = None
        for s in range(subgrids):
            first = dot(low_ref[...], seen_ref[slot, s, 0])
            second = dot(low_ref[...], seen_ref[slot, s, 1])
            real = first[:pair_rows] + second[pair_rows:]
            imag = second[:pair_rows] - first[pair_rows:]
            back = [
                jnp.broadcast_to(down_ref[i, h, pl.ds(base, pair_rows), s : s + 1], (pair_rows, size))
                for h in (0, 1)
            ]
            term = times((real, imag), (back[0], -back[1]))
            sums = term if sums is None else (sums[0] + term[0], sums[1] + term[1])
        part = slice(i * pair_rows, (i + 1) * pair_rows) if isinstance(i, int) else pl.ds(
            pl.multiple_of(i * pair_rows, pair_rows), pair_rows
        )
        gathered_ref[part, :size] = sums[0].astype(BF16)
        gathered_ref[part, size:] = sums[1].astype(BF16)

    lift(0, 0)
    for i in range(mine_columns):
        one_column(i, i % 2, i + 1 if i + 1 < mine_columns else None)

    first = dot(gathered_ref[:, :size], wa_ref[...])
    second = dot(gathered_ref[:, size:], wa_ref[...])
    real = first[:, :slab] - second[:, slab:]
    imag = first[:, slab:] + second[:, :slab]
    total = None
    for i in range(mine_columns):
        part = slice(i * pair_rows, (i + 1) * pair_rows)
        back_real = jnp.broadcast_to(phase_ref[i * 2 * ROWS : i * 2 * ROWS + 1], (pair_rows, slab))
        back_imag = jnp.broadcast_to(
            phase_ref[i * 2 * ROWS + ROWS : i * 2 * ROWS + ROWS + 1], (pair_rows, slab)
        )
        term = times((real[part], imag[part]), (back_real, -back_imag))
        total = term if total is None else (total[0] + term[0], total[1] + term[1])
    both = jnp.concatenate(total, axis=1)
    mine_ref[...] = jnp.where(core == 0, both[:local], both[local:])
    other_ref[...] = jnp.where(core == 0, both[local:], both[:local])


def pair_body(facets, sub_offsets, col_offsets, screen_index, screens):
    facet_count = lax.axis_size("facet")
    column_count = lax.axis_size("col")
    devices = facet_count * column_count
    local_rows, slab = facets.shape[1], facets.shape[3]
    height = local_rows * column_count
    rows = facet_count * height
    subgrid_count = sub_offsets.shape[1]
    size = screens.shape[2]
    span = -(-(XC + STEP * (facet_count - 1)) // LANES) * LANES
    dims = (facet_count, height, span, slab, size, column_count, local_rows)
    any_space = pl.BlockSpec(memory_space=pl.ANY)
    smem = pl.BlockSpec(memory_space=pltpu.MemorySpace.SMEM)
    width = 2 * slab + LANES

    outgoing = pl.pallas_call(
        pair_send_kernel,
        out_shape=jax.ShapeDtypeStruct((devices, local_rows, width), BF16),
        in_specs=[any_space, any_space, smem, smem],
        out_specs=pl.BlockSpec(memory_space=VMEM),
        scratch_shapes=[
            pltpu.VMEM(facets.shape, BF16),
            pltpu.SMEM(sub_offsets.shape, jnp.int32),
            pltpu.SemaphoreType.DMA((2,)),
        ],
        compiler_params=pltpu.CompilerParams(vmem_limit_bytes=VMEM_LIMIT),
        name="send",
    )(in_hbm(facets), in_hbm(sub_offsets), col_offsets, screen_index)
    everyone = lax.all_to_all(
        outgoing, ("facet", "col"), split_axis=0, concat_axis=0, tiled=True
    ).reshape(rows, width)
    table_shapes = [
        ((facet_count, 2 * span, 2 * slab), BF16),
        ((2 * size, rows), BF16),
        ((2 * span, 2 * size), BF16),
        ((4 * local_rows, size), BF16),
        ((size, 2 * slab), BF16),
        (screens.shape, F32),
    ]
    table_bytes = sum(math.prod(s) * jnp.dtype(t).itemsize for s, t in table_shapes)
    tables = pl.pallas_call(
        functools.partial(pair_tables_kernel, dims),
        out_shape=[jax.ShapeDtypeStruct(s, t) for s, t in table_shapes],
        in_specs=[any_space],
        out_specs=whole(len(table_shapes)),
        scratch_shapes=[pltpu.SemaphoreType.DMA],
        compiler_params=pltpu.CompilerParams(vmem_limit_bytes=VMEM_LIMIT),
        cost_estimate=pl.CostEstimate(
            flops=100 * table_bytes, bytes_accessed=2 * table_bytes, transcendentals=0
        ),
        name="tables",
    )(in_hbm(screens))
    mine, other = pl.pallas_call(
        functools.partial(pair_kernel, dims),
        out_shape=[jax.ShapeDtypeStruct((local_rows, 2 * slab), F32)] * 2,
        in_specs=whole(1 + len(tables)),
        out_specs=whole(2),
        scratch_shapes=[
            pltpu.VMEM((ROWS, rows), jnp.int32),
            pltpu.SMEM((ROWS, rows), jnp.int32),
            pltpu.VMEM((column_count // 2, rows, 2 * span), F32),
            pltpu.VMEM((column_count // 2, 2, rows, LANES), F32),
            pltpu.VMEM((2, subgrid_count * size, 2 * span), BF16),
            pltpu.VMEM((2, subgrid_count, rows, 2 * span), BF16),
            pltpu.VMEM((2, subgrid_count, 2, size, size), BF16),
            pltpu.VMEM((column_count * local_rows, 2 * size), BF16),
            pltpu.VMEM((column_count * ROWS, slab), F32),
            pltpu.SemaphoreType.DMA,
        ],
        compiler_params=pltpu.CompilerParams(vmem_limit_bytes=VMEM_LIMIT),
        name="window",
    )(everyone, *tables)
    swap = [(i, i ^ 1) for i in range(column_count)]
    summed = mine + lax.ppermute(other, "col", swap)
    return (summed / math.sqrt(column_count * subgrid_count)).reshape(1, local_rows, 2, slab)


def send_kernel(facets_ref, out_ref, mine_ref, sem):
    copy = pltpu.make_async_copy(facets_ref, mine_ref, sem)
    copy.start()
    copy.wait()
    mine = jnp.concatenate([mine_ref[0, :, 0, :], mine_ref[0, :, 1, :]], axis=1)
    out_ref[...] = jnp.broadcast_to(mine[None], out_ref.shape)


def in_hbm(array):
    return pltpu.with_memory_space_constraint(array, pltpu.MemorySpace.HBM)


def whole(count):
    return [pl.BlockSpec(memory_space=VMEM)] * count


def spread_body(facets, sub_offsets, col_offsets, screen_index, screens):
    axes = ("facet", "col")
    facet_count = lax.axis_size("facet")
    column_count = lax.axis_size("col")
    devices = facet_count * column_count
    local_rows, slab = facets.shape[1], facets.shape[3]
    height = local_rows * column_count
    rows = facet_count * height
    subgrid_count = sub_offsets.shape[1]
    owned = subgrid_count // facet_count
    size = screens.shape[2]
    span = -(-(XC + STEP * (facet_count - 1)) // LANES) * LANES
    chunk = max(height, min(rows, CHUNK))
    dims = (facet_count, height, span, slab, size, owned, chunk)

    outgoing = pl.pallas_call(
        send_kernel,
        out_shape=jax.ShapeDtypeStruct((devices, local_rows, 2 * slab), BF16),
        in_specs=[pl.BlockSpec(memory_space=pl.ANY)],
        out_specs=pl.BlockSpec(memory_space=VMEM),
        scratch_shapes=[pltpu.VMEM(facets.shape, BF16), pltpu.SemaphoreType.DMA],
        compiler_params=pltpu.CompilerParams(vmem_limit_bytes=VMEM_LIMIT),
        name="send",
    )(in_hbm(facets))
    everyone = lax.all_to_all(outgoing, axes, split_axis=0, concat_axis=0, tiled=True)
    everyone = everyone.reshape(rows, 2 * slab)
    numbers = jnp.concatenate([col_offsets, screen_index[0], sub_offsets[0]])
    table_shapes = [
        ((facet_count, 2 * slab, 2 * span), BF16),
        ((owned, 2 * size, rows), BF16),
        ((2 * span, 2 * size), BF16),
        ((size, 2 * span), BF16),
        ((owned, rows, 2 * size), BF16),
        ((facet_count, 2 * span, 2 * slab), BF16),
        ((owned, 2, size, size), F32),
    ]
    table_bytes = sum(math.prod(s) * jnp.dtype(t).itemsize for s, t in table_shapes)
    tables = pl.pallas_call(
        functools.partial(tables_kernel, dims),
        out_shape=[jax.ShapeDtypeStruct(s, t) for s, t in table_shapes],
        in_specs=[pl.BlockSpec(memory_space=pl.ANY)] * 2,
        out_specs=whole(len(table_shapes)),
        scratch_shapes=[
            pltpu.SMEM(numbers.shape, jnp.int32),
            pltpu.SemaphoreType.DMA,
            pltpu.SemaphoreType.DMA((owned,)),
        ],
        compiler_params=pltpu.CompilerParams(vmem_limit_bytes=VMEM_LIMIT),
        cost_estimate=pl.CostEstimate(
            flops=100 * table_bytes, bytes_accessed=2 * table_bytes, transcendentals=0
        ),
        name="tables",
    )(numbers, in_hbm(screens))
    terms = pl.pallas_call(
        functools.partial(main_kernel, dims),
        out_shape=jax.ShapeDtypeStruct((rows, 2 * slab), BF16),
        in_specs=whole(1 + len(tables)),
        out_specs=pl.BlockSpec(memory_space=VMEM),
        scratch_shapes=[pltpu.VMEM((rows, 2 * span), BF16)],
        compiler_params=pltpu.CompilerParams(vmem_limit_bytes=VMEM_LIMIT),
        name="window",
    )(everyone, *tables)
    terms = terms.reshape(devices, local_rows, 2 * slab)
    arrived = lax.all_to_all(terms, axes, split_axis=0, concat_axis=0, tiled=True)
    factor = 1.0 / math.sqrt(column_count * subgrid_count)
    summed = jnp.sum(arrived.astype(F32), axis=0) * factor
    return summed.reshape(1, local_rows, 2, slab)


def body(facets, sub_offsets, col_offsets, screen_index, screens):
    columns, subgrids = lax.axis_size("col"), sub_offsets.shape[1]
    alone = columns % 2 == 0 and subgrids == lax.axis_size("facet") and columns * subgrids <= 32
    run = pair_body if alone else spread_body
    return run(facets, sub_offsets, col_offsets, screen_index, screens)


def solution(mesh):
    return jax.shard_map(
        body,
        mesh=mesh,
        in_specs=(P("facet", "col", None, None), P("col", None), P("col"), P("col", "facet"), P()),
        out_specs=P("facet", "col", None, None),
        check_vma=False,
    )
```

```python
import functools
import math

import jax
import jax.numpy as jnp
from jax import lax
from jax.experimental import pallas as pl
from jax.experimental.pallas import tpu as pltpu
from jax.sharding import PartitionSpec as P

XC = 64
NPAD = 8192
STEP = 7
ROWS = 8
LANES = 128
CHUNK = 256
HALF = 7
UNROLL = False
VMEM_LIMIT = 24 * 2**20
F32 = jnp.float32
BF16 = jnp.bfloat16
VMEM = pltpu.MemorySpace.VMEM


def wave(number, period, scale):
    quarter = period // 4
    bits = quarter.bit_length() - 1
    turn = (number + quarter // 2) >> bits
    angle = (number - (turn << bits)).astype(F32) * (2.0 * math.pi / period)
    square = angle * angle
    sine = angle * (1.0 + square * (-1 / 6 + square * (1 / 120 + square * (-1 / 5040))))
    cosine = 1.0 + square * (-1 / 2 + square * (1 / 24 + square * (-1 / 720 + square * (1 / 40320))))
    odd = (turn & 1) == 1
    first = jnp.where(odd, sine, cosine)
    second = jnp.where(odd, cosine, sine)
    first = jnp.where(((turn + 1) & 2) == 2, -scale, scale) * first
    second = jnp.where((turn & 2) == 2, -scale, scale) * second
    return first, second


def each(count, step):
    if count == 1:
        step(0)
    else:
        lax.fori_loop(0, count, lambda i, c: (step(i), c)[1], 0)


def iota(shape, axis):
    return lax.broadcasted_iota(jnp.int32, shape, axis)


def ladder(first, step, count):
    real, imag = first
    reals, imags = [real], [imag]
    for _ in range(count - 1):
        real, imag = real * step[0] - imag * step[1], real * step[1] + imag * step[0]
        reals.append(real)
        imags.append(imag)
    return jnp.concatenate(reals, axis=0), jnp.concatenate(imags, axis=0)


def fourier(rows, row_start, lane_numbers, period, scale):
    shape = (ROWS, lane_numbers.shape[1])
    lanes = jnp.broadcast_to(lane_numbers, shape) & (period - 1)
    top = (iota(shape, 0) + row_start) & (period - 1)
    first = wave((top * lanes) & (period - 1), period, scale)
    return ladder(first, wave((ROWS * lanes) & (period - 1), period, 1.0), rows // ROWS)


def block(real, imag, flip):
    low, high = (imag, -imag) if flip else (-imag, imag)
    return jnp.concatenate(
        [jnp.concatenate([real, high], axis=1), jnp.concatenate([low, real], axis=1)], axis=0
    )


def tables_kernel(
    dims, numbers_hbm, screens_ref,
    a_ref, wp_ref, wt_ref, w_ref, wph_ref, ah_ref, gain_ref,
    numbers_ref, small_sem, sem,
):
    facets, height, span, slab, size, owned, chunk = dims
    rows = facets * height
    small = pltpu.make_async_copy(numbers_hbm, numbers_ref, small_sem)
    small.start()

    scale = 1.0 / math.sqrt(size)
    real, imag = fourier(size, 0, iota((1, span), 1), size, scale)
    w_real, w_imag = real.astype(BF16), imag.astype(BF16)
    w_both = jnp.concatenate([w_real, w_imag], axis=1)
    w_ref[...] = w_both
    real, imag = fourier(span, 0, iota((1, size), 1), size, scale)
    wt_ref[...] = block(real.astype(BF16), imag.astype(BF16), False)

    small.wait()
    copies = [
        pltpu.make_async_copy(screens_ref.at[numbers_ref[1 + k]], gain_ref.at[k], sem.at[k])
        for k in range(owned)
    ]
    for copy in copies:
        copy.start()
    column = numbers_ref[0]

    def facet_tables(f):
        lag = STEP * f
        lanes = iota((1, span), 1) - lag
        scale = 1.0 / math.sqrt(slab)
        real, imag = fourier(slab, 0, column + lanes, NPAD, scale / math.sqrt(facets))
        inside = jnp.broadcast_to((lanes >= 0) & (lanes < XC), real.shape)
        zero = jnp.zeros_like(real)
        a_ref[f] = block(
            jnp.where(inside, real, zero).astype(BF16),
            jnp.where(inside, -imag, zero).astype(BF16),
            False,
        )
        real, imag = fourier(span, column - lag, iota((1, slab), 1), NPAD, scale)
        down = iota(real.shape, 0) - lag
        inside = (down >= 0) & (down < XC)
        zero = jnp.zeros_like(real)
        ah_ref[f] = block(
            jnp.where(inside, real, zero).astype(BF16),
            jnp.where(inside, -imag, zero).astype(BF16),
            True,
        )

    if rows == chunk:
        for f in range(facets):
            facet_tables(f)
    else:
        each(facets, facet_tables)

    first = 1 + owned + lax.axis_index("facet") * owned
    scale = 1.0 / math.sqrt(height)
    shift = height.bit_length() - 1

    def row_chunk(k, i):
        fixed = isinstance(i, int)
        base = i * chunk

        def along(start):
            return pl.ds(start, chunk) if fixed else pl.ds(pl.multiple_of(start, chunk), chunk)

        offset = numbers_ref[first + k]
        row = iota((1, chunk), 1) + base
        lag = STEP * (row >> shift)
        low = jnp.broadcast_to((offset - lag) & (NPAD - 1), (ROWS, chunk))
        lanes = jnp.broadcast_to(row & (NPAD - 1), (ROWS, chunk))
        top = (low + iota((ROWS, chunk), 0)) & (NPAD - 1)
        real, imag = ladder(
            wave((top * lanes) & (NPAD - 1), NPAD, scale),
            wave((ROWS * lanes) & (NPAD - 1), NPAD, 1.0),
            span // ROWS,
        )
        u = iota((span, chunk), 0) - lag
        inside = (u >= 0) & (u < XC)
        zero = jnp.zeros_like(real)
        real = jnp.where(inside, real, zero).astype(BF16)
        imag = jnp.where(inside, -imag, zero).astype(BF16)
        both = dot(w_both, block(real, imag, False)).astype(BF16)
        wp_ref[k, :size, along(base)] = both[:, :chunk]
        wp_ref[k, size:, along(base)] = both[:, chunk:]
        reals, imags = [], []
        for f in range(chunk // height):
            lag = STEP * ((base >> shift) + f)
            lanes = iota((1, span), 1) - lag
            real, imag = fourier(height, base + f * height, lanes + offset, NPAD, scale)
            inside = jnp.broadcast_to((lanes >= 0) & (lanes < XC), real.shape)
            zero = jnp.zeros_like(real)
            reals.append(jnp.where(inside, real, zero).astype(BF16))
            imags.append(jnp.where(inside, -imag, zero).astype(BF16))
        both = jnp.concatenate(
            [jnp.concatenate(reals, axis=0), jnp.concatenate(imags, axis=0)], axis=1
        )
        wph_ref[k, along(base), :] = dot(both, wt_ref[...]).astype(BF16)

    for k in range(owned):
        each(rows // chunk, functools.partial(row_chunk, k))
    for copy in copies:
        copy.wait()


def dot(first, second):
    return jnp.dot(first, second, preferred_element_type=F32)


def main_kernel(
    dims, x_ref, a_ref, wp_ref, wt_ref, w_ref, wph_ref, ah_ref, gain_ref, out_ref, spread_ref,
):
    facets, height, span, slab, size, owned, chunk = dims
    rows = facets * height

    def by_facet(value, i, table_ref):
        parts = []
        for f in range(chunk // height):
            own = value[f * height : (f + 1) * height]
            parts.append(dot(own, table_ref[i * (chunk // height) + f]).astype(BF16))
        return parts[0] if len(parts) == 1 else jnp.concatenate(parts, axis=0)

    def along(i):
        base = i * chunk
        return pl.ds(base, chunk) if isinstance(i, int) else pl.ds(pl.multiple_of(base, chunk), chunk)

    def spread(i):
        spread_ref[along(i), :] = by_facet(x_ref[along(i), :], i, a_ref)

    each(rows // chunk, spread)
    inners = []
    for k in range(owned):
        first = dot(wp_ref[k, :size], spread_ref[...])
        second = dot(wp_ref[k, size:], spread_ref[...])
        half = jnp.concatenate(
            [first[:, :span] - second[:, span:], first[:, span:] + second[:, :span]], axis=1
        ).astype(BF16)
        grid = dot(half, wt_ref[...])
        real, imag = grid[:, :size], grid[:, size:]
        gain_real, gain_imag = gain_ref[k, 0], gain_ref[k, 1]
        seen_real = (real * gain_real - imag * gain_imag).astype(BF16)
        seen_imag = (real * gain_imag + imag * gain_real).astype(BF16)
        first = dot(seen_real, w_ref[...])
        second = dot(seen_imag, w_ref[...])
        inners.append(
            jnp.concatenate(
                [first[:, :span] + second[:, span:], second[:, :span] - first[:, span:]], axis=1
            ).astype(BF16)
        )

    def back(i):
        own = 0.0
        for k in range(owned):
            first = dot(wph_ref[k, along(i), :size], inners[k])
            second = dot(wph_ref[k, along(i), size:], inners[k])
            own += jnp.concatenate(
                [first[:, :span] + second[:, span:], first[:, span:] - second[:, :span]], axis=1
            )
        out_ref[along(i), :] = by_facet(own.astype(BF16), i, ah_ref)

    each(rows // chunk, back)


def pair_send_kernel(facets_ref, sub_hbm, col_ref, pick_ref, out_ref, mine_ref, sub_ref, sem):
    copies = [
        pltpu.make_async_copy(facets_ref, mine_ref, sem.at[0]),
        pltpu.make_async_copy(sub_hbm, sub_ref, sem.at[1]),
    ]
    for copy in copies:
        copy.start()
    for copy in copies:
        copy.wait()
    numbers = (col_ref[0], sub_ref[0, lax.axis_index("facet")], pick_ref[0, 0])
    shape = (1, 2, out_ref.shape[3])
    lane, low = iota(shape, 2), iota(shape, 1) == 1
    told = jnp.zeros(shape, jnp.int32)
    for i, number in enumerate(numbers):
        value = jnp.where(low, number & ((1 << HALF) - 1), number >> HALF)
        told = jnp.where(lane == i, value, told)
    mine = jnp.concatenate([mine_ref[0], told.astype(F32).astype(BF16)], axis=0)
    out_ref[...] = jnp.broadcast_to(mine[None], out_ref.shape)


def fine_dot(first, second):
    parts = []
    for value in (first, second):
        high = value.astype(BF16)
        parts.append((high, (value - high.astype(F32)).astype(BF16)))
    (a, a_rest), (b, b_rest) = parts
    return dot(a, b) + (dot(a, b_rest) + dot(a_rest, b))


def pair_tables_kernel(
    dims, screens_hbm, a_ref, wp_ref, wt_ref, low_ref, wa_ref, screens_ref, sem
):
    facets, height, span, slab, size, columns, local = dims
    rows = facets * height
    copy = pltpu.make_async_copy(screens_hbm, screens_ref, sem)
    copy.start()
    scale = 1.0 / math.sqrt(size)
    w_both = jnp.concatenate(fourier(size, 0, iota((1, span), 1), size, scale), axis=1)
    w_turned = block(*fourier(span, 0, iota((1, size), 1), size, scale), False)
    wt_ref[...] = w_turned.astype(BF16)

    def keep(number, real, imag):
        inside = jnp.broadcast_to((number >= 0) & (number < XC), real.shape)
        zero = jnp.zeros_like(real)
        return jnp.where(inside, real, zero), jnp.where(inside, -imag, zero)

    facet = lax.axis_index("facet")
    lag = STEP * facet
    scale = 1.0 / math.sqrt(slab)
    for f in range(facets):
        lanes = iota((1, span), 1) - STEP * f
        real, imag = keep(lanes, *fourier(slab, 0, lanes, NPAD, scale / math.sqrt(facets)))
        a_ref[f] = block(real.astype(BF16), imag.astype(BF16), False)
    real, imag = fourier(span, -lag, iota((1, slab), 1), NPAD, scale)
    both = fine_dot(w_both, block(*keep(iota(real.shape, 0) - lag, real, imag), False))
    wa_ref[:, :slab] = both[:, :slab].astype(BF16)
    wa_ref[:, slab:] = (-both[:, slab:]).astype(BF16)

    scale = 1.0 / math.sqrt(height)
    row = iota((1, rows), 1)
    behind = STEP * (row >> (height.bit_length() - 1))
    lanes = jnp.broadcast_to(row & (NPAD - 1), (ROWS, rows))
    top = (jnp.broadcast_to(-behind, (ROWS, rows)) + iota((ROWS, rows), 0)) & (NPAD - 1)
    real, imag = ladder(
        wave((top * lanes) & (NPAD - 1), NPAD, scale),
        wave((ROWS * lanes) & (NPAD - 1), NPAD, 1.0),
        span // ROWS,
    )
    both = fine_dot(w_both, block(*keep(iota(real.shape, 0) - behind, real, imag), False)).astype(BF16)
    wp_ref[:size] = both[:, :rows]
    wp_ref[size:] = both[:, rows:]

    pair_rows = 2 * local
    base = facet * height + (lax.axis_index("col") >> 1) * pair_rows
    lanes = iota((1, span), 1) - lag
    real, imag = keep(lanes, *fourier(pair_rows, base, lanes, NPAD, scale))
    both = fine_dot(jnp.concatenate([real, imag], axis=1), w_turned).astype(BF16)
    low_ref[:pair_rows] = both[:, :size]
    low_ref[pair_rows:] = both[:, size:]
    copy.wait()


def dot_nt(first, second):
    return lax.dot_general(first, second, (((1,), (1,)), ((), ())), preferred_element_type=F32)


def pair_kernel(
    dims, x_ref, a_ref, wp_ref, wt_ref, low_ref, wa_ref, screens_ref, mine_ref, other_ref,
    wide_ref, told_ref, numbers_ref, spread_ref, down_ref, half_ref, lifted_ref, seen_ref, gathered_ref, phase_ref, sem,
):
    facets, height, span, slab, size, columns, local = dims
    rows = facets * height
    subgrids = facets
    pair_rows = 2 * local
    mine_columns = columns // 2
    core = lax.axis_index("col") & 1
    base = lax.axis_index("facet") * height + (lax.axis_index("col") >> 1) * pair_rows

    pitch = 2 * (local + 1)
    devices = x_ref.shape[0] // pitch
    wide_ref[...] = x_ref[...].astype(F32)
    told = [
        jnp.concatenate(
            [wide_ref[k * pitch + 2 * local + h : k * pitch + 2 * local + h + 1] for k in range(devices)],
            axis=0,
        )
        for h in (0, 1)
    ]
    told_ref[...] = (told[0] * (1 << HALF) + told[1]).astype(jnp.int32)
    copy = pltpu.make_async_copy(told_ref, numbers_ref, sem)
    copy.start()

    def number(kind, facet, column):
        return numbers_ref[facet * columns + column, kind]

    def spread_number(kind, facet, column, shape):
        own = told_ref[pl.ds(facet * columns + column, 1), :]
        return jnp.broadcast_to(own[:, kind : kind + 1], shape)

    def times(a, b):
        return a[0] * b[0] - a[1] * b[1], a[0] * b[1] + a[1] * b[0]

    def phases(offset, where):
        real, imag = wave((where * offset) & (NPAD - 1), NPAD, 1.0)
        return real, -imag

    own = [
        jnp.concatenate(
            [wide_ref[pl.ds(k * pitch + h, local, stride=2), :] for k in range(devices)], axis=0
        )
        for h in (0, 1)
    ]
    for i in range(mine_columns):
        column = 2 * i + core
        ahead = phases(spread_number(0, 0, column, (ROWS, slab)), iota((ROWS, slab), 1))
        phase_ref[2 * i * ROWS : (2 * i + 1) * ROWS, :] = ahead[0]
        phase_ref[(2 * i + 1) * ROWS : (2 * i + 2) * ROWS, :] = ahead[1]
        line = iota((ROWS, rows), 0)
        offset_rows = jnp.zeros((ROWS, rows), jnp.int32)
        for s in range(subgrids):
            offset_rows = jnp.where(line == s, spread_number(1, s, column, line.shape), offset_rows)
        row_phase = phases(offset_rows, iota((ROWS, rows), 1))
        for h in (0, 1):
            down_ref[i, h, :, :ROWS] = row_phase[h].T
        real, imag = times(
            own,
            [jnp.broadcast_to(p[:1], (rows, slab)) for p in ahead],
        )
        turned = jnp.concatenate([real.astype(BF16), imag.astype(BF16)], axis=1)
        for f in range(facets):
            part = slice(f * height, (f + 1) * height)
            spread_ref[i, part, :] = dot(turned[part], a_ref[f])

    def lift(i, slot):
        for s in range(subgrids):
            down = [jnp.broadcast_to(down_ref[i, h, :, s : s + 1], (rows, span)) for h in (0, 1)]
            real, imag = times((spread_ref[i, :, :span], spread_ref[i, :, span:]), down)
            lifted_ref[slot, s, :, :span] = real.astype(BF16)
            lifted_ref[slot, s, :, span:] = imag.astype(BF16)

    def one_column(i, slot, following):
        for s in range(subgrids):
            lifted = lifted_ref[slot, s]
            first = dot(wp_ref[:size], lifted)
            second = dot(wp_ref[size:], lifted)
            part = slice(s * size, (s + 1) * size)
            half_ref[slot, part, :span] = (first[:, :span] - second[:, span:]).astype(BF16)
            half_ref[slot, part, span:] = (first[:, span:] + second[:, :span]).astype(BF16)
        if following is not None:
            lift(following, 1 - slot)
        half = half_ref[slot]
        all_real, all_imag = dot(half, wt_ref[:, :size]), dot(half, wt_ref[:, size:])
        for s in range(subgrids):
            part = slice(s * size, (s + 1) * size)
            real, imag = all_real[part], all_imag[part]
            pick = number(2, s, 2 * i + core)
            gain_real, gain_imag = screens_ref[pick, 0], screens_ref[pick, 1]
            seen_ref[slot, s, 0] = (real * gain_real - imag * gain_imag).astype(BF16)
            seen_ref[slot, s, 1] = (real * gain_imag + imag * gain_real).astype(BF16)
        sums = None
        for s in range(subgrids):
            first = dot(low_ref[...], seen_ref[slot, s, 0])
            second = dot(low_ref[...], seen_ref[slot, s, 1])
            real = first[:pair_rows] + second[pair_rows:]
            imag = second[:pair_rows] - first[pair_rows:]
            back = [
                jnp.broadcast_to(down_ref[i, h, pl.ds(base, pair_rows), s : s + 1], (pair_rows, size))
                for h in (0, 1)
            ]
            term = times((real, imag), (back[0], -back[1]))
            sums = term if sums is None else (sums[0] + term[0], sums[1] + term[1])
        part = slice(i * pair_rows, (i + 1) * pair_rows) if isinstance(i, int) else pl.ds(
            pl.multiple_of(i * pair_rows, pair_rows), pair_rows
        )
        gathered_ref[part, :size] = sums[0].astype(BF16)
        gathered_ref[part, size:] = sums[1].astype(BF16)

    lift(0, 0)
    copy.wait()
    for i in range(mine_columns):
        one_column(i, i % 2, i + 1 if i + 1 < mine_columns else None)

    first = dot(gathered_ref[:, :size], wa_ref[...])
    second = dot(gathered_ref[:, size:], wa_ref[...])
    real = first[:, :slab] - second[:, slab:]
    imag = first[:, slab:] + second[:, :slab]
    total = None
    for i in range(mine_columns):
        part = slice(i * pair_rows, (i + 1) * pair_rows)
        back_real = jnp.broadcast_to(phase_ref[i * 2 * ROWS : i * 2 * ROWS + 1], (pair_rows, slab))
        back_imag = jnp.broadcast_to(
            phase_ref[i * 2 * ROWS + ROWS : i * 2 * ROWS + ROWS + 1], (pair_rows, slab)
        )
        term = times((real[part], imag[part]), (back_real, -back_imag))
        total = term if total is None else (total[0] + term[0], total[1] + term[1])
    both = jnp.concatenate(total, axis=1)
    mine_ref[...] = jnp.where(core == 0, both[:local], both[local:])
    other_ref[...] = jnp.where(core == 0, both[local:], both[:local])


def pair_body(facets, sub_offsets, col_offsets, screen_index, screens):
    facet_count = lax.axis_size("facet")
    column_count = lax.axis_size("col")
    devices = facet_count * column_count
    local_rows, slab = facets.shape[1], facets.shape[3]
    height = local_rows * column_count
    rows = facet_count * height
    subgrid_count = sub_offsets.shape[1]
    size = screens.shape[2]
    span = -(-(XC + STEP * (facet_count - 1)) // LANES) * LANES
    dims = (facet_count, height, span, slab, size, column_count, local_rows)
    any_space = pl.BlockSpec(memory_space=pl.ANY)
    smem = pl.BlockSpec(memory_space=pltpu.MemorySpace.SMEM)

    outgoing = pl.pallas_call(
        pair_send_kernel,
        out_shape=jax.ShapeDtypeStruct((devices, local_rows + 1, 2, slab), BF16),
        in_specs=[any_space, any_space, smem, smem],
        out_specs=pl.BlockSpec(memory_space=VMEM),
        scratch_shapes=[
            pltpu.VMEM(facets.shape, BF16),
            pltpu.SMEM(sub_offsets.shape, jnp.int32),
            pltpu.SemaphoreType.DMA((2,)),
        ],
        compiler_params=pltpu.CompilerParams(vmem_limit_bytes=VMEM_LIMIT),
        name="send",
    )(in_hbm(facets), in_hbm(sub_offsets), col_offsets, screen_index)
    everyone = lax.all_to_all(
        outgoing, ("facet", "col"), split_axis=0, concat_axis=0, tiled=True
    ).reshape(devices * (local_rows + 1) * 2, slab)
    table_shapes = [
        ((facet_count, 2 * span, 2 * slab), BF16),
        ((2 * size, rows), BF16),
        ((2 * span, 2 * size), BF16),
        ((4 * local_rows, size), BF16),
        ((size, 2 * slab), BF16),
        (screens.shape, F32),
    ]
    table_bytes = sum(math.prod(s) * jnp.dtype(t).itemsize for s, t in table_shapes)
    tables = pl.pallas_call(
        functools.partial(pair_tables_kernel, dims),
        out_shape=[jax.ShapeDtypeStruct(s, t) for s, t in table_shapes],
        in_specs=[any_space],
        out_specs=whole(len(table_shapes)),
        scratch_shapes=[pltpu.SemaphoreType.DMA],
        compiler_params=pltpu.CompilerParams(vmem_limit_bytes=VMEM_LIMIT),
        cost_estimate=pl.CostEstimate(
            flops=100 * table_bytes, bytes_accessed=2 * table_bytes, transcendentals=0
        ),
        name="tables",
    )(in_hbm(screens))
    mine, other = pl.pallas_call(
        functools.partial(pair_kernel, dims),
        out_shape=[jax.ShapeDtypeStruct((local_rows, 2 * slab), F32)] * 2,
        in_specs=whole(1 + len(tables)),
        out_specs=whole(2),
        scratch_shapes=[
            pltpu.VMEM(everyone.shape, F32),
            pltpu.VMEM((devices, slab), jnp.int32),
            pltpu.SMEM((devices, slab), jnp.int32),
            pltpu.VMEM((column_count // 2, rows, 2 * span), F32),
            pltpu.VMEM((column_count // 2, 2, rows, LANES), F32),
            pltpu.VMEM((2, subgrid_count * size, 2 * span), BF16),
            pltpu.VMEM((2, subgrid_count, rows, 2 * span), BF16),
            pltpu.VMEM((2, subgrid_count, 2, size, size), BF16),
            pltpu.VMEM((column_count * local_rows, 2 * size), BF16),
            pltpu.VMEM((column_count * ROWS, slab), F32),
            pltpu.SemaphoreType.DMA,
        ],
        compiler_params=pltpu.CompilerParams(vmem_limit_bytes=VMEM_LIMIT),
        name="window",
    )(everyone, *tables)
    swap = [(i, i ^ 1) for i in range(column_count)]
    summed = mine + lax.ppermute(other, "col", swap)
    return (summed / math.sqrt(column_count * subgrid_count)).reshape(1, local_rows, 2, slab)


def send_kernel(facets_ref, out_ref, mine_ref, sem):
    copy = pltpu.make_async_copy(facets_ref, mine_ref, sem)
    copy.start()
    copy.wait()
    mine = jnp.concatenate([mine_ref[0, :, 0, :], mine_ref[0, :, 1, :]], axis=1)
    out_ref[...] = jnp.broadcast_to(mine[None], out_ref.shape)


def in_hbm(array):
    return pltpu.with_memory_space_constraint(array, pltpu.MemorySpace.HBM)


def whole(count):
    return [pl.BlockSpec(memory_space=VMEM)] * count


def spread_body(facets, sub_offsets, col_offsets, screen_index, screens):
    axes = ("facet", "col")
    facet_count = lax.axis_size("facet")
    column_count = lax.axis_size("col")
    devices = facet_count * column_count
    local_rows, slab = facets.shape[1], facets.shape[3]
    height = local_rows * column_count
    rows = facet_count * height
    subgrid_count = sub_offsets.shape[1]
    owned = subgrid_count // facet_count
    size = screens.shape[2]
    span = -(-(XC + STEP * (facet_count - 1)) // LANES) * LANES
    chunk = max(height, min(rows, CHUNK))
    dims = (facet_count, height, span, slab, size, owned, chunk)

    outgoing = pl.pallas_call(
        send_kernel,
        out_shape=jax.ShapeDtypeStruct((devices, local_rows, 2 * slab), BF16),
        in_specs=[pl.BlockSpec(memory_space=pl.ANY)],
        out_specs=pl.BlockSpec(memory_space=VMEM),
        scratch_shapes=[pltpu.VMEM(facets.shape, BF16), pltpu.SemaphoreType.DMA],
        compiler_params=pltpu.CompilerParams(vmem_limit_bytes=VMEM_LIMIT),
        name="send",
    )(in_hbm(facets))
    everyone = lax.all_to_all(outgoing, axes, split_axis=0, concat_axis=0, tiled=True)
    everyone = everyone.reshape(rows, 2 * slab)
    numbers = jnp.concatenate([col_offsets, screen_index[0], sub_offsets[0]])
    table_shapes = [
        ((facet_count, 2 * slab, 2 * span), BF16),
        ((owned, 2 * size, rows), BF16),
        ((2 * span, 2 * size), BF16),
        ((size, 2 * span), BF16),
        ((owned, rows, 2 * size), BF16),
        ((facet_count, 2 * span, 2 * slab), BF16),
        ((owned, 2, size, size), F32),
    ]
    table_bytes = sum(math.prod(s) * jnp.dtype(t).itemsize for s, t in table_shapes)
    tables = pl.pallas_call(
        functools.partial(tables_kernel, dims),
        out_shape=[jax.ShapeDtypeStruct(s, t) for s, t in table_shapes],
        in_specs=[pl.BlockSpec(memory_space=pl.ANY)] * 2,
        out_specs=whole(len(table_shapes)),
        scratch_shapes=[
            pltpu.SMEM(numbers.shape, jnp.int32),
            pltpu.SemaphoreType.DMA,
            pltpu.SemaphoreType.DMA((owned,)),
        ],
        compiler_params=pltpu.CompilerParams(vmem_limit_bytes=VMEM_LIMIT),
        cost_estimate=pl.CostEstimate(
            flops=100 * table_bytes, bytes_accessed=2 * table_bytes, transcendentals=0
        ),
        name="tables",
    )(numbers, in_hbm(screens))
    terms = pl.pallas_call(
        functools.partial(main_kernel, dims),
        out_shape=jax.ShapeDtypeStruct((rows, 2 * slab), BF16),
        in_specs=whole(1 + len(tables)),
        out_specs=pl.BlockSpec(memory_space=VMEM),
        scratch_shapes=[pltpu.VMEM((rows, 2 * span), BF16)],
        compiler_params=pltpu.CompilerParams(vmem_limit_bytes=VMEM_LIMIT),
        name="window",
    )(everyone, *tables)
    terms = terms.reshape(devices, local_rows, 2 * slab)
    arrived = lax.all_to_all(terms, axes, split_axis=0, concat_axis=0, tiled=True)
    factor = 1.0 / math.sqrt(column_count * subgrid_count)
    summed = jnp.sum(arrived.astype(F32), axis=0) * factor
    return summed.reshape(1, local_rows, 2, slab)


def body(facets, sub_offsets, col_offsets, screen_index, screens):
    columns, subgrids = lax.axis_size("col"), sub_offsets.shape[1]
    alone = columns % 2 == 0 and subgrids == lax.axis_size("facet") and columns * subgrids <= 32
    run = pair_body if alone else spread_body
    return run(facets, sub_offsets, col_offsets, screen_index, screens)


def solution(mesh):
    return jax.shard_map(
        body,
        mesh=mesh,
        in_specs=(P("facet", "col", None, None), P("col", None), P("col"), P("col", "facet"), P()),
        out_specs=P("facet", "col", None, None),
        check_vma=False,
    )
```

```python
import functools
import math

import jax
import jax.numpy as jnp
from jax import lax
from jax.experimental import pallas as pl
from jax.experimental.pallas import tpu as pltpu
from jax.sharding import PartitionSpec as P

XC = 64
NPAD = 8192
STEP = 7
ROWS = 8
LANES = 128
CHUNK = 256
HALF = 7
VMEM_LIMIT = 24 * 2**20
F32 = jnp.float32
BF16 = jnp.bfloat16
VMEM = pltpu.MemorySpace.VMEM


def wave(number, period, scale):
    quarter = period // 4
    bits = quarter.bit_length() - 1
    turn = (number + quarter // 2) >> bits
    angle = (number - (turn << bits)).astype(F32) * (2.0 * math.pi / period)
    square = angle * angle
    sine = angle * (1.0 + square * (-1 / 6 + square * (1 / 120 + square * (-1 / 5040))))
    cosine = 1.0 + square * (-1 / 2 + square * (1 / 24 + square * (-1 / 720 + square * (1 / 40320))))
    odd = (turn & 1) == 1
    first = jnp.where(odd, sine, cosine)
    second = jnp.where(odd, cosine, sine)
    first = jnp.where(((turn + 1) & 2) == 2, -scale, scale) * first
    second = jnp.where((turn & 2) == 2, -scale, scale) * second
    return first, second


def each(count, step):
    if count == 1:
        step(0)
    else:
        lax.fori_loop(0, count, lambda i, c: (step(i), c)[1], 0)


def iota(shape, axis):
    return lax.broadcasted_iota(jnp.int32, shape, axis)


def ladder(first, step, count):
    real, imag = first
    reals, imags = [real], [imag]
    for _ in range(count - 1):
        real, imag = real * step[0] - imag * step[1], real * step[1] + imag * step[0]
        reals.append(real)
        imags.append(imag)
    return jnp.concatenate(reals, axis=0), jnp.concatenate(imags, axis=0)


def fourier(rows, row_start, lane_numbers, period, scale):
    shape = (ROWS, lane_numbers.shape[1])
    lanes = jnp.broadcast_to(lane_numbers, shape) & (period - 1)
    top = (iota(shape, 0) + row_start) & (period - 1)
    first = wave((top * lanes) & (period - 1), period, scale)
    return ladder(first, wave((ROWS * lanes) & (period - 1), period, 1.0), rows // ROWS)


def block(real, imag, flip):
    low, high = (imag, -imag) if flip else (-imag, imag)
    return jnp.concatenate(
        [jnp.concatenate([real, high], axis=1), jnp.concatenate([low, real], axis=1)], axis=0
    )


def tables_kernel(
    dims, numbers_hbm, screens_ref,
    a_ref, wp_ref, wt_ref, w_ref, wph_ref, ah_ref, gain_ref,
    numbers_ref, small_sem, sem,
):
    facets, height, span, slab, size, owned, chunk = dims
    rows = facets * height
    small = pltpu.make_async_copy(numbers_hbm, numbers_ref, small_sem)
    small.start()

    scale = 1.0 / math.sqrt(size)
    real, imag = fourier(size, 0, iota((1, span), 1), size, scale)
    w_real, w_imag = real.astype(BF16), imag.astype(BF16)
    w_both = jnp.concatenate([w_real, w_imag], axis=1)
    w_ref[...] = w_both
    real, imag = fourier(span, 0, iota((1, size), 1), size, scale)
    wt_ref[...] = block(real.astype(BF16), imag.astype(BF16), False)

    small.wait()
    copies = [
        pltpu.make_async_copy(screens_ref.at[numbers_ref[1 + k]], gain_ref.at[k], sem.at[k])
        for k in range(owned)
    ]
    for copy in copies:
        copy.start()
    column = numbers_ref[0]

    def facet_tables(f):
        lag = STEP * f
        lanes = iota((1, span), 1) - lag
        scale = 1.0 / math.sqrt(slab)
        real, imag = fourier(slab, 0, column + lanes, NPAD, scale / math.sqrt(facets))
        inside = jnp.broadcast_to((lanes >= 0) & (lanes < XC), real.shape)
        zero = jnp.zeros_like(real)
        a_ref[f] = block(
            jnp.where(inside, real, zero).astype(BF16),
            jnp.where(inside, -imag, zero).astype(BF16),
            False,
        )
        real, imag = fourier(span, column - lag, iota((1, slab), 1), NPAD, scale)
        down = iota(real.shape, 0) - lag
        inside = (down >= 0) & (down < XC)
        zero = jnp.zeros_like(real)
        ah_ref[f] = block(
            jnp.where(inside, real, zero).astype(BF16),
            jnp.where(inside, -imag, zero).astype(BF16),
            True,
        )

    if rows == chunk:
        for f in range(facets):
            facet_tables(f)
    else:
        each(facets, facet_tables)

    first = 1 + owned + lax.axis_index("facet") * owned
    scale = 1.0 / math.sqrt(height)
    shift = height.bit_length() - 1

    def row_chunk(k, i):
        fixed = isinstance(i, int)
        base = i * chunk

        def along(start):
            return pl.ds(start, chunk) if fixed else pl.ds(pl.multiple_of(start, chunk), chunk)

        offset = numbers_ref[first + k]
        row = iota((1, chunk), 1) + base
        lag = STEP * (row >> shift)
        low = jnp.broadcast_to((offset - lag) & (NPAD - 1), (ROWS, chunk))
        lanes = jnp.broadcast_to(row & (NPAD - 1), (ROWS, chunk))
        top = (low + iota((ROWS, chunk), 0)) & (NPAD - 1)
        real, imag = ladder(
            wave((top * lanes) & (NPAD - 1), NPAD, scale),
            wave((ROWS * lanes) & (NPAD - 1), NPAD, 1.0),
            span // ROWS,
        )
        u = iota((span, chunk), 0) - lag
        inside = (u >= 0) & (u < XC)
        zero = jnp.zeros_like(real)
        real = jnp.where(inside, real, zero).astype(BF16)
        imag = jnp.where(inside, -imag, zero).astype(BF16)
        both = dot(w_both, block(real, imag, False)).astype(BF16)
        wp_ref[k, :size, along(base)] = both[:, :chunk]
        wp_ref[k, size:, along(base)] = both[:, chunk:]
        reals, imags = [], []
        for f in range(chunk // height):
            lag = STEP * ((base >> shift) + f)
            lanes = iota((1, span), 1) - lag
            real, imag = fourier(height, base + f * height, lanes + offset, NPAD, scale)
            inside = jnp.broadcast_to((lanes >= 0) & (lanes < XC), real.shape)
            zero = jnp.zeros_like(real)
            reals.append(jnp.where(inside, real, zero).astype(BF16))
            imags.append(jnp.where(inside, -imag, zero).astype(BF16))
        both = jnp.concatenate(
            [jnp.concatenate(reals, axis=0), jnp.concatenate(imags, axis=0)], axis=1
        )
        wph_ref[k, along(base), :] = dot(both, wt_ref[...]).astype(BF16)

    for k in range(owned):
        each(rows // chunk, functools.partial(row_chunk, k))
    for copy in copies:
        copy.wait()


def dot(first, second):
    return jnp.dot(first, second, preferred_element_type=F32)


def main_kernel(
    dims, x_ref, a_ref, wp_ref, wt_ref, w_ref, wph_ref, ah_ref, gain_ref, out_ref, spread_ref,
):
    facets, height, span, slab, size, owned, chunk = dims
    rows = facets * height

    def by_facet(value, i, table_ref):
        parts = []
        for f in range(chunk // height):
            own = value[f * height : (f + 1) * height]
            parts.append(dot(own, table_ref[i * (chunk // height) + f]).astype(BF16))
        return parts[0] if len(parts) == 1 else jnp.concatenate(parts, axis=0)

    def along(i):
        base = i * chunk
        return pl.ds(base, chunk) if isinstance(i, int) else pl.ds(pl.multiple_of(base, chunk), chunk)

    def spread(i):
        spread_ref[along(i), :] = by_facet(x_ref[along(i), :], i, a_ref)

    each(rows // chunk, spread)
    inners = []
    for k in range(owned):
        first = dot(wp_ref[k, :size], spread_ref[...])
        second = dot(wp_ref[k, size:], spread_ref[...])
        half = jnp.concatenate(
            [first[:, :span] - second[:, span:], first[:, span:] + second[:, :span]], axis=1
        ).astype(BF16)
        grid = dot(half, wt_ref[...])
        real, imag = grid[:, :size], grid[:, size:]
        gain_real, gain_imag = gain_ref[k, 0], gain_ref[k, 1]
        seen_real = (real * gain_real - imag * gain_imag).astype(BF16)
        seen_imag = (real * gain_imag + imag * gain_real).astype(BF16)
        first = dot(seen_real, w_ref[...])
        second = dot(seen_imag, w_ref[...])
        inners.append(
            jnp.concatenate(
                [first[:, :span] + second[:, span:], second[:, :span] - first[:, span:]], axis=1
            ).astype(BF16)
        )

    def back(i):
        own = 0.0
        for k in range(owned):
            first = dot(wph_ref[k, along(i), :size], inners[k])
            second = dot(wph_ref[k, along(i), size:], inners[k])
            own += jnp.concatenate(
                [first[:, :span] + second[:, span:], first[:, span:] - second[:, :span]], axis=1
            )
        out_ref[along(i), :] = by_facet(own.astype(BF16), i, ah_ref)

    each(rows // chunk, back)


def pair_send_kernel(facets_ref, sub_hbm, col_ref, pick_ref, out_ref, mine_ref, sub_ref, sem):
    copies = [
        pltpu.make_async_copy(facets_ref, mine_ref, sem.at[0]),
        pltpu.make_async_copy(sub_hbm, sub_ref, sem.at[1]),
    ]
    for copy in copies:
        copy.start()
    for copy in copies:
        copy.wait()
    numbers = (col_ref[0], sub_ref[0, lax.axis_index("facet")], pick_ref[0, 0])
    shape = (1, 2, out_ref.shape[3])
    lane, low = iota(shape, 2), iota(shape, 1) == 1
    told = jnp.zeros(shape, jnp.int32)
    for i, number in enumerate(numbers):
        value = jnp.where(low, number & ((1 << HALF) - 1), number >> HALF)
        told = jnp.where(lane == i, value, told)
    mine = jnp.concatenate([mine_ref[0], told.astype(F32).astype(BF16)], axis=0)
    out_ref[...] = jnp.broadcast_to(mine[None], out_ref.shape)


def fine_dot(first, second):
    parts = []
    for value in (first, second):
        high = value.astype(BF16)
        parts.append((high, (value - high.astype(F32)).astype(BF16)))
    (a, a_rest), (b, b_rest) = parts
    return dot(a, b) + (dot(a, b_rest) + dot(a_rest, b))


def pair_tables_kernel(
    dims, screens_hbm, a_ref, wp_ref, wt_ref, low_ref, wa_ref, screens_ref, sem
):
    facets, height, span, slab, size, columns, local = dims
    rows = facets * height
    copy = pltpu.make_async_copy(screens_hbm, screens_ref, sem)
    copy.start()
    scale = 1.0 / math.sqrt(size)
    w_both = jnp.concatenate(fourier(size, 0, iota((1, span), 1), size, scale), axis=1)
    w_turned = block(*fourier(span, 0, iota((1, size), 1), size, scale), False)
    wt_ref[...] = w_turned.astype(BF16)

    def keep(number, real, imag):
        inside = jnp.broadcast_to((number >= 0) & (number < XC), real.shape)
        zero = jnp.zeros_like(real)
        return jnp.where(inside, real, zero), jnp.where(inside, -imag, zero)

    facet = lax.axis_index("facet")
    lag = STEP * facet
    scale = 1.0 / math.sqrt(slab)
    for f in range(facets):
        lanes = iota((1, span), 1) - STEP * f
        real, imag = keep(lanes, *fourier(slab, 0, lanes, NPAD, scale / math.sqrt(facets)))
        a_ref[f] = block(real.astype(BF16), imag.astype(BF16), False)
    real, imag = fourier(span, -lag, iota((1, slab), 1), NPAD, scale)
    both = fine_dot(w_both, block(*keep(iota(real.shape, 0) - lag, real, imag), False))
    wa_ref[:, :slab] = both[:, :slab].astype(BF16)
    wa_ref[:, slab:] = (-both[:, slab:]).astype(BF16)

    scale = 1.0 / math.sqrt(height)
    row = iota((1, rows), 1)
    behind = STEP * (row >> (height.bit_length() - 1))
    lanes = jnp.broadcast_to(row & (NPAD - 1), (ROWS, rows))
    top = (jnp.broadcast_to(-behind, (ROWS, rows)) + iota((ROWS, rows), 0)) & (NPAD - 1)
    real, imag = ladder(
        wave((top * lanes) & (NPAD - 1), NPAD, scale),
        wave((ROWS * lanes) & (NPAD - 1), NPAD, 1.0),
        span // ROWS,
    )
    both = fine_dot(w_both, block(*keep(iota(real.shape, 0) - behind, real, imag), False)).astype(BF16)
    wp_ref[:size] = both[:, :rows]
    wp_ref[size:] = both[:, rows:]

    pair_rows = 2 * local
    base = facet * height + (lax.axis_index("col") >> 1) * pair_rows
    lanes = iota((1, span), 1) - lag
    real, imag = keep(lanes, *fourier(pair_rows, base, lanes, NPAD, scale))
    both = fine_dot(jnp.concatenate([real, imag], axis=1), w_turned).astype(BF16)
    low_ref[:pair_rows] = both[:, :size]
    low_ref[pair_rows:] = both[:, size:]
    copy.wait()


def dot_nt(first, second):
    return lax.dot_general(first, second, (((1,), (1,)), ((), ())), preferred_element_type=F32)


def pair_kernel(
    dims, x_ref, a_ref, wp_ref, wt_ref, low_ref, wa_ref, screens_ref, mine_ref, other_ref,
    wide_ref, told_ref, numbers_ref, spread_ref, down_ref, half_ref, lifted_ref, seen_ref, gathered_ref, phase_ref, sem,
):
    facets, height, span, slab, size, columns, local = dims
    rows = facets * height
    subgrids = facets
    pair_rows = 2 * local
    mine_columns = columns // 2
    core = lax.axis_index("col") & 1
    base = lax.axis_index("facet") * height + (lax.axis_index("col") >> 1) * pair_rows

    pitch = 2 * (local + 1)
    devices = x_ref.shape[0] // pitch
    wide_ref[...] = x_ref[...].astype(F32)
    told = [
        jnp.concatenate(
            [wide_ref[k * pitch + 2 * local + h : k * pitch + 2 * local + h + 1] for k in range(devices)],
            axis=0,
        )
        for h in (0, 1)
    ]
    told_ref[...] = (told[0] * (1 << HALF) + told[1]).astype(jnp.int32)
    copy = pltpu.make_async_copy(told_ref, numbers_ref, sem)
    copy.start()

    def number(kind, facet, column):
        return numbers_ref[facet * columns + column, kind]

    def spread_number(kind, facet, column, shape):
        own = told_ref[pl.ds(facet * columns + column, 1), :]
        return jnp.broadcast_to(own[:, kind : kind + 1], shape)

    def times(a, b):
        return a[0] * b[0] - a[1] * b[1], a[0] * b[1] + a[1] * b[0]

    def phases(offset, where):
        real, imag = wave((where * offset) & (NPAD - 1), NPAD, 1.0)
        return real, -imag

    own = [
        jnp.concatenate(
            [wide_ref[pl.ds(k * pitch + h, local, stride=2), :] for k in range(devices)], axis=0
        )
        for h in (0, 1)
    ]
    for i in range(mine_columns):
        column = 2 * i + core
        ahead = phases(spread_number(0, 0, column, (ROWS, slab)), iota((ROWS, slab), 1))
        phase_ref[2 * i * ROWS : (2 * i + 1) * ROWS, :] = ahead[0]
        phase_ref[(2 * i + 1) * ROWS : (2 * i + 2) * ROWS, :] = ahead[1]
        line = iota((ROWS, rows), 0)
        offset_rows = jnp.zeros((ROWS, rows), jnp.int32)
        for s in range(subgrids):
            offset_rows = jnp.where(line == s, spread_number(1, s, column, line.shape), offset_rows)
        row_phase = phases(offset_rows, iota((ROWS, rows), 1))
        for h in (0, 1):
            down_ref[i, h, :, :ROWS] = row_phase[h].T
        real, imag = times(
            own,
            [jnp.broadcast_to(p[:1], (rows, slab)) for p in ahead],
        )
        turned = jnp.concatenate([real.astype(BF16), imag.astype(BF16)], axis=1)
        for f in range(facets):
            part = slice(f * height, (f + 1) * height)
            spread_ref[i, part, :] = dot(turned[part], a_ref[f])

    def lift(i, slot):
        for s in range(subgrids):
            down = [jnp.broadcast_to(down_ref[i, h, :, s : s + 1], (rows, span)) for h in (0, 1)]
            real, imag = times((spread_ref[i, :, :span], spread_ref[i, :, span:]), down)
            lifted_ref[slot, s, :, :span] = real.astype(BF16)
            lifted_ref[slot, s, :, span:] = imag.astype(BF16)

    def halve(slot):
        for s in range(subgrids):
            lifted = lifted_ref[slot, s]
            first = dot(wp_ref[:size], lifted)
            second = dot(wp_ref[size:], lifted)
            part = slice(s * size, (s + 1) * size)
            half_ref[slot, part, :span] = (first[:, :span] - second[:, span:]).astype(BF16)
            half_ref[slot, part, span:] = (first[:, span:] + second[:, :span]).astype(BF16)

    def one_column(i, slot, following):
        if following is not None:
            halve(1 - slot)
        if following is not None and following + 1 < mine_columns:
            lift(following + 1, slot)
        half = half_ref[slot]
        all_real, all_imag = dot(half, wt_ref[:, :size]), dot(half, wt_ref[:, size:])
        for s in range(subgrids):
            part = slice(s * size, (s + 1) * size)
            real, imag = all_real[part], all_imag[part]
            pick = number(2, s, 2 * i + core)
            gain_real, gain_imag = screens_ref[pick, 0], screens_ref[pick, 1]
            seen_ref[slot, s, 0] = (real * gain_real - imag * gain_imag).astype(BF16)
            seen_ref[slot, s, 1] = (real * gain_imag + imag * gain_real).astype(BF16)
        sums = None
        for s in range(subgrids):
            first = dot(low_ref[...], seen_ref[slot, s, 0])
            second = dot(low_ref[...], seen_ref[slot, s, 1])
            real = first[:pair_rows] + second[pair_rows:]
            imag = second[:pair_rows] - first[pair_rows:]
            back = [
                jnp.broadcast_to(down_ref[i, h, pl.ds(base, pair_rows), s : s + 1], (pair_rows, size))
                for h in (0, 1)
            ]
            term = times((real, imag), (back[0], -back[1]))
            sums = term if sums is None else (sums[0] + term[0], sums[1] + term[1])
        part = slice(i * pair_rows, (i + 1) * pair_rows) if isinstance(i, int) else pl.ds(
            pl.multiple_of(i * pair_rows, pair_rows), pair_rows
        )
        gathered_ref[part, :size] = sums[0].astype(BF16)
        gathered_ref[part, size:] = sums[1].astype(BF16)

    lift(0, 0)
    halve(0)
    lift(1, 1)
    copy.wait()
    for i in range(mine_columns):
        one_column(i, i % 2, i + 1 if i + 1 < mine_columns else None)

    first = dot(gathered_ref[:, :size], wa_ref[...])
    second = dot(gathered_ref[:, size:], wa_ref[...])
    real = first[:, :slab] - second[:, slab:]
    imag = first[:, slab:] + second[:, :slab]
    total = None
    for i in range(mine_columns):
        part = slice(i * pair_rows, (i + 1) * pair_rows)
        back_real = jnp.broadcast_to(phase_ref[i * 2 * ROWS : i * 2 * ROWS + 1], (pair_rows, slab))
        back_imag = jnp.broadcast_to(
            phase_ref[i * 2 * ROWS + ROWS : i * 2 * ROWS + ROWS + 1], (pair_rows, slab)
        )
        term = times((real[part], imag[part]), (back_real, -back_imag))
        total = term if total is None else (total[0] + term[0], total[1] + term[1])
    both = jnp.concatenate(total, axis=1)
    mine_ref[...] = jnp.where(core == 0, both[:local], both[local:])
    other_ref[...] = jnp.where(core == 0, both[local:], both[:local])


def pair_body(facets, sub_offsets, col_offsets, screen_index, screens):
    facet_count = lax.axis_size("facet")
    column_count = lax.axis_size("col")
    devices = facet_count * column_count
    local_rows, slab = facets.shape[1], facets.shape[3]
    height = local_rows * column_count
    rows = facet_count * height
    subgrid_count = sub_offsets.shape[1]
    size = screens.shape[2]
    span = -(-(XC + STEP * (facet_count - 1)) // LANES) * LANES
    dims = (facet_count, height, span, slab, size, column_count, local_rows)
    any_space = pl.BlockSpec(memory_space=pl.ANY)
    smem = pl.BlockSpec(memory_space=pltpu.MemorySpace.SMEM)

    outgoing = pl.pallas_call(
        pair_send_kernel,
        out_shape=jax.ShapeDtypeStruct((devices, local_rows + 1, 2, slab), BF16),
        in_specs=[any_space, any_space, smem, smem],
        out_specs=pl.BlockSpec(memory_space=VMEM),
        scratch_shapes=[
            pltpu.VMEM(facets.shape, BF16),
            pltpu.SMEM(sub_offsets.shape, jnp.int32),
            pltpu.SemaphoreType.DMA((2,)),
        ],
        compiler_params=pltpu.CompilerParams(vmem_limit_bytes=VMEM_LIMIT),
        name="send",
    )(in_hbm(facets), in_hbm(sub_offsets), col_offsets, screen_index)
    everyone = lax.all_to_all(
        outgoing, ("facet", "col"), split_axis=0, concat_axis=0, tiled=True
    ).reshape(devices * (local_rows + 1) * 2, slab)
    table_shapes = [
        ((facet_count, 2 * span, 2 * slab), BF16),
        ((2 * size, rows), BF16),
        ((2 * span, 2 * size), BF16),
        ((4 * local_rows, size), BF16),
        ((size, 2 * slab), BF16),
        (screens.shape, F32),
    ]
    table_bytes = sum(math.prod(s) * jnp.dtype(t).itemsize for s, t in table_shapes)
    tables = pl.pallas_call(
        functools.partial(pair_tables_kernel, dims),
        out_shape=[jax.ShapeDtypeStruct(s, t) for s, t in table_shapes],
        in_specs=[any_space],
        out_specs=whole(len(table_shapes)),
        scratch_shapes=[pltpu.SemaphoreType.DMA],
        compiler_params=pltpu.CompilerParams(vmem_limit_bytes=VMEM_LIMIT),
        cost_estimate=pl.CostEstimate(
            flops=100 * table_bytes, bytes_accessed=2 * table_bytes, transcendentals=0
        ),
        name="tables",
    )(in_hbm(screens))
    mine, other = pl.pallas_call(
        functools.partial(pair_kernel, dims),
        out_shape=[jax.ShapeDtypeStruct((local_rows, 2 * slab), F32)] * 2,
        in_specs=whole(1 + len(tables)),
        out_specs=whole(2),
        scratch_shapes=[
            pltpu.VMEM(everyone.shape, F32),
            pltpu.VMEM((devices, slab), jnp.int32),
            pltpu.SMEM((devices, slab), jnp.int32),
            pltpu.VMEM((column_count // 2, rows, 2 * span), F32),
            pltpu.VMEM((column_count // 2, 2, rows, LANES), F32),
            pltpu.VMEM((2, subgrid_count * size, 2 * span), BF16),
            pltpu.VMEM((2, subgrid_count, rows, 2 * span), BF16),
            pltpu.VMEM((2, subgrid_count, 2, size, size), BF16),
            pltpu.VMEM((column_count * local_rows, 2 * size), BF16),
            pltpu.VMEM((column_count * ROWS, slab), F32),
            pltpu.SemaphoreType.DMA,
        ],
        compiler_params=pltpu.CompilerParams(vmem_limit_bytes=VMEM_LIMIT),
        name="window",
    )(everyone, *tables)
    swap = [(i, i ^ 1) for i in range(column_count)]
    summed = mine + lax.ppermute(other, "col", swap)
    return (summed / math.sqrt(column_count * subgrid_count)).reshape(1, local_rows, 2, slab)


def send_kernel(facets_ref, out_ref, mine_ref, sem):
    copy = pltpu.make_async_copy(facets_ref, mine_ref, sem)
    copy.start()
    copy.wait()
    mine = jnp.concatenate([mine_ref[0, :, 0, :], mine_ref[0, :, 1, :]], axis=1)
    out_ref[...] = jnp.broadcast_to(mine[None], out_ref.shape)


def in_hbm(array):
    return pltpu.with_memory_space_constraint(array, pltpu.MemorySpace.HBM)


def whole(count):
    return [pl.BlockSpec(memory_space=VMEM)] * count


def spread_body(facets, sub_offsets, col_offsets, screen_index, screens):
    axes = ("facet", "col")
    facet_count = lax.axis_size("facet")
    column_count = lax.axis_size("col")
    devices = facet_count * column_count
    local_rows, slab = facets.shape[1], facets.shape[3]
    height = local_rows * column_count
    rows = facet_count * height
    subgrid_count = sub_offsets.shape[1]
    owned = subgrid_count // facet_count
    size = screens.shape[2]
    span = -(-(XC + STEP * (facet_count - 1)) // LANES) * LANES
    chunk = max(height, min(rows, CHUNK))
    dims = (facet_count, height, span, slab, size, owned, chunk)

    outgoing = pl.pallas_call(
        send_kernel,
        out_shape=jax.ShapeDtypeStruct((devices, local_rows, 2 * slab), BF16),
        in_specs=[pl.BlockSpec(memory_space=pl.ANY)],
        out_specs=pl.BlockSpec(memory_space=VMEM),
        scratch_shapes=[pltpu.VMEM(facets.shape, BF16), pltpu.SemaphoreType.DMA],
        compiler_params=pltpu.CompilerParams(vmem_limit_bytes=VMEM_LIMIT),
        name="send",
    )(in_hbm(facets))
    everyone = lax.all_to_all(outgoing, axes, split_axis=0, concat_axis=0, tiled=True)
    everyone = everyone.reshape(rows, 2 * slab)
    numbers = jnp.concatenate([col_offsets, screen_index[0], sub_offsets[0]])
    table_shapes = [
        ((facet_count, 2 * slab, 2 * span), BF16),
        ((owned, 2 * size, rows), BF16),
        ((2 * span, 2 * size), BF16),
        ((size, 2 * span), BF16),
        ((owned, rows, 2 * size), BF16),
        ((facet_count, 2 * span, 2 * slab), BF16),
        ((owned, 2, size, size), F32),
    ]
    table_bytes = sum(math.prod(s) * jnp.dtype(t).itemsize for s, t in table_shapes)
    tables = pl.pallas_call(
        functools.partial(tables_kernel, dims),
        out_shape=[jax.ShapeDtypeStruct(s, t) for s, t in table_shapes],
        in_specs=[pl.BlockSpec(memory_space=pl.ANY)] * 2,
        out_specs=whole(len(table_shapes)),
        scratch_shapes=[
            pltpu.SMEM(numbers.shape, jnp.int32),
            pltpu.SemaphoreType.DMA,
            pltpu.SemaphoreType.DMA((owned,)),
        ],
        compiler_params=pltpu.CompilerParams(vmem_limit_bytes=VMEM_LIMIT),
        cost_estimate=pl.CostEstimate(
            flops=100 * table_bytes, bytes_accessed=2 * table_bytes, transcendentals=0
        ),
        name="tables",
    )(numbers, in_hbm(screens))
    terms = pl.pallas_call(
        functools.partial(main_kernel, dims),
        out_shape=jax.ShapeDtypeStruct((rows, 2 * slab), BF16),
        in_specs=whole(1 + len(tables)),
        out_specs=pl.BlockSpec(memory_space=VMEM),
        scratch_shapes=[pltpu.VMEM((rows, 2 * span), BF16)],
        compiler_params=pltpu.CompilerParams(vmem_limit_bytes=VMEM_LIMIT),
        name="window",
    )(everyone, *tables)
    terms = terms.reshape(devices, local_rows, 2 * slab)
    arrived = lax.all_to_all(terms, axes, split_axis=0, concat_axis=0, tiled=True)
    factor = 1.0 / math.sqrt(column_count * subgrid_count)
    summed = jnp.sum(arrived.astype(F32), axis=0) * factor
    return summed.reshape(1, local_rows, 2, slab)


def body(facets, sub_offsets, col_offsets, screen_index, screens):
    columns, subgrids = lax.axis_size("col"), sub_offsets.shape[1]
    alone = columns % 4 == 0 and subgrids == lax.axis_size("facet") and columns * subgrids <= 32
    run = pair_body if alone else spread_body
    return run(facets, sub_offsets, col_offsets, screen_index, screens)


def solution(mesh):
    return jax.shard_map(
        body,
        mesh=mesh,
        in_specs=(P("facet", "col", None, None), P("col", None), P("col"), P("col", "facet"), P()),
        out_specs=P("facet", "col", None, None),
        check_vma=False,
    )
```

```python
import functools
import math

import jax
import jax.numpy as jnp
from jax import lax
from jax.experimental import pallas as pl
from jax.experimental.pallas import tpu as pltpu
from jax.sharding import PartitionSpec as P

XC = 64
NPAD = 8192
STEP = 7
ROWS = 8
LANES = 128
CHUNK = 256
HALF = 7
VMEM_LIMIT = 24 * 2**20
F32 = jnp.float32
BF16 = jnp.bfloat16
VMEM = pltpu.MemorySpace.VMEM


def wave(number, period, scale):
    quarter = period // 4
    bits = quarter.bit_length() - 1
    turn = (number + quarter // 2) >> bits
    angle = (number - (turn << bits)).astype(F32) * (2.0 * math.pi / period)
    square = angle * angle
    sine = angle * (1.0 + square * (-1 / 6 + square * (1 / 120 + square * (-1 / 5040))))
    cosine = 1.0 + square * (-1 / 2 + square * (1 / 24 + square * (-1 / 720 + square * (1 / 40320))))
    odd = (turn & 1) == 1
    first = jnp.where(odd, sine, cosine)
    second = jnp.where(odd, cosine, sine)
    first = jnp.where(((turn + 1) & 2) == 2, -scale, scale) * first
    second = jnp.where((turn & 2) == 2, -scale, scale) * second
    return first, second


def each(count, step):
    if count == 1:
        step(0)
    else:
        lax.fori_loop(0, count, lambda i, c: (step(i), c)[1], 0)


def iota(shape, axis):
    return lax.broadcasted_iota(jnp.int32, shape, axis)


def ladder(first, step, count):
    real, imag = first
    reals, imags = [real], [imag]
    for _ in range(count - 1):
        real, imag = real * step[0] - imag * step[1], real * step[1] + imag * step[0]
        reals.append(real)
        imags.append(imag)
    return jnp.concatenate(reals, axis=0), jnp.concatenate(imags, axis=0)


def fourier(rows, row_start, lane_numbers, period, scale):
    shape = (ROWS, lane_numbers.shape[1])
    lanes = jnp.broadcast_to(lane_numbers, shape) & (period - 1)
    top = (iota(shape, 0) + row_start) & (period - 1)
    first = wave((top * lanes) & (period - 1), period, scale)
    return ladder(first, wave((ROWS * lanes) & (period - 1), period, 1.0), rows // ROWS)


def block(real, imag, flip):
    low, high = (imag, -imag) if flip else (-imag, imag)
    return jnp.concatenate(
        [jnp.concatenate([real, high], axis=1), jnp.concatenate([low, real], axis=1)], axis=0
    )


def tables_kernel(
    dims, numbers_hbm, screens_ref,
    a_ref, wp_ref, wt_ref, w_ref, wph_ref, ah_ref, gain_ref,
    numbers_ref, small_sem, sem,
):
    facets, height, span, slab, size, owned, chunk = dims
    rows = facets * height
    small = pltpu.make_async_copy(numbers_hbm, numbers_ref, small_sem)
    small.start()

    scale = 1.0 / math.sqrt(size)
    real, imag = fourier(size, 0, iota((1, span), 1), size, scale)
    w_real, w_imag = real.astype(BF16), imag.astype(BF16)
    w_both = jnp.concatenate([w_real, w_imag], axis=1)
    w_ref[...] = w_both
    real, imag = fourier(span, 0, iota((1, size), 1), size, scale)
    wt_ref[...] = block(real.astype(BF16), imag.astype(BF16), False)

    small.wait()
    copies = [
        pltpu.make_async_copy(screens_ref.at[numbers_ref[1 + k]], gain_ref.at[k], sem.at[k])
        for k in range(owned)
    ]
    for copy in copies:
        copy.start()
    column = numbers_ref[0]

    def facet_tables(f):
        lag = STEP * f
        lanes = iota((1, span), 1) - lag
        scale = 1.0 / math.sqrt(slab)
        real, imag = fourier(slab, 0, column + lanes, NPAD, scale / math.sqrt(facets))
        inside = jnp.broadcast_to((lanes >= 0) & (lanes < XC), real.shape)
        zero = jnp.zeros_like(real)
        a_ref[f] = block(
            jnp.where(inside, real, zero).astype(BF16),
            jnp.where(inside, -imag, zero).astype(BF16),
            False,
        )
        real, imag = fourier(span, column - lag, iota((1, slab), 1), NPAD, scale)
        down = iota(real.shape, 0) - lag
        inside = (down >= 0) & (down < XC)
        zero = jnp.zeros_like(real)
        ah_ref[f] = block(
            jnp.where(inside, real, zero).astype(BF16),
            jnp.where(inside, -imag, zero).astype(BF16),
            True,
        )

    if rows == chunk:
        for f in range(facets):
            facet_tables(f)
    else:
        each(facets, facet_tables)

    first = 1 + owned + lax.axis_index("facet") * owned
    scale = 1.0 / math.sqrt(height)
    shift = height.bit_length() - 1

    def row_chunk(k, i):
        fixed = isinstance(i, int)
        base = i * chunk

        def along(start):
            return pl.ds(start, chunk) if fixed else pl.ds(pl.multiple_of(start, chunk), chunk)

        offset = numbers_ref[first + k]
        row = iota((1, chunk), 1) + base
        lag = STEP * (row >> shift)
        low = jnp.broadcast_to((offset - lag) & (NPAD - 1), (ROWS, chunk))
        lanes = jnp.broadcast_to(row & (NPAD - 1), (ROWS, chunk))
        top = (low + iota((ROWS, chunk), 0)) & (NPAD - 1)
        real, imag = ladder(
            wave((top * lanes) & (NPAD - 1), NPAD, scale),
            wave((ROWS * lanes) & (NPAD - 1), NPAD, 1.0),
            span // ROWS,
        )
        u = iota((span, chunk), 0) - lag
        inside = (u >= 0) & (u < XC)
        zero = jnp.zeros_like(real)
        real = jnp.where(inside, real, zero).astype(BF16)
        imag = jnp.where(inside, -imag, zero).astype(BF16)
        both = dot(w_both, block(real, imag, False)).astype(BF16)
        wp_ref[k, :size, along(base)] = both[:, :chunk]
        wp_ref[k, size:, along(base)] = both[:, chunk:]
        reals, imags = [], []
        for f in range(chunk // height):
            lag = STEP * ((base >> shift) + f)
            lanes = iota((1, span), 1) - lag
            real, imag = fourier(height, base + f * height, lanes + offset, NPAD, scale)
            inside = jnp.broadcast_to((lanes >= 0) & (lanes < XC), real.shape)
            zero = jnp.zeros_like(real)
            reals.append(jnp.where(inside, real, zero).astype(BF16))
            imags.append(jnp.where(inside, -imag, zero).astype(BF16))
        both = jnp.concatenate(
            [jnp.concatenate(reals, axis=0), jnp.concatenate(imags, axis=0)], axis=1
        )
        wph_ref[k, along(base), :] = dot(both, wt_ref[...]).astype(BF16)

    for k in range(owned):
        each(rows // chunk, functools.partial(row_chunk, k))
    for copy in copies:
        copy.wait()


def dot(first, second):
    return jnp.dot(first, second, preferred_element_type=F32)


def main_kernel(
    dims, x_ref, a_ref, wp_ref, wt_ref, w_ref, wph_ref, ah_ref, gain_ref, out_ref, spread_ref,
):
    facets, height, span, slab, size, owned, chunk = dims
    rows = facets * height

    def by_facet(value, i, table_ref):
        parts = []
        for f in range(chunk // height):
            own = value[f * height : (f + 1) * height]
            parts.append(dot(own, table_ref[i * (chunk // height) + f]).astype(BF16))
        return parts[0] if len(parts) == 1 else jnp.concatenate(parts, axis=0)

    def along(i):
        base = i * chunk
        return pl.ds(base, chunk) if isinstance(i, int) else pl.ds(pl.multiple_of(base, chunk), chunk)

    def spread(i):
        spread_ref[along(i), :] = by_facet(x_ref[along(i), :], i, a_ref)

    each(rows // chunk, spread)
    inners = []
    for k in range(owned):
        first = dot(wp_ref[k, :size], spread_ref[...])
        second = dot(wp_ref[k, size:], spread_ref[...])
        half = jnp.concatenate(
            [first[:, :span] - second[:, span:], first[:, span:] + second[:, :span]], axis=1
        ).astype(BF16)
        grid = dot(half, wt_ref[...])
        real, imag = grid[:, :size], grid[:, size:]
        gain_real, gain_imag = gain_ref[k, 0], gain_ref[k, 1]
        seen_real = (real * gain_real - imag * gain_imag).astype(BF16)
        seen_imag = (real * gain_imag + imag * gain_real).astype(BF16)
        first = dot(seen_real, w_ref[...])
        second = dot(seen_imag, w_ref[...])
        inners.append(
            jnp.concatenate(
                [first[:, :span] + second[:, span:], second[:, :span] - first[:, span:]], axis=1
            ).astype(BF16)
        )

    def back(i):
        own = 0.0
        for k in range(owned):
            first = dot(wph_ref[k, along(i), :size], inners[k])
            second = dot(wph_ref[k, along(i), size:], inners[k])
            own += jnp.concatenate(
                [first[:, :span] + second[:, span:], first[:, span:] - second[:, :span]], axis=1
            )
        out_ref[along(i), :] = by_facet(own.astype(BF16), i, ah_ref)

    each(rows // chunk, back)


def pair_send_kernel(facets_ref, sub_hbm, col_ref, pick_ref, out_ref, mine_ref, sub_ref, sem):
    copies = [
        pltpu.make_async_copy(facets_ref, mine_ref, sem.at[0]),
        pltpu.make_async_copy(sub_hbm, sub_ref, sem.at[1]),
    ]
    for copy in copies:
        copy.start()
    for copy in copies:
        copy.wait()
    numbers = (col_ref[0], sub_ref[0, lax.axis_index("facet")], pick_ref[0, 0])
    shape = (1, 2, out_ref.shape[3])
    lane, low = iota(shape, 2), iota(shape, 1) == 1
    told = jnp.zeros(shape, jnp.int32)
    for i, number in enumerate(numbers):
        value = jnp.where(low, number & ((1 << HALF) - 1), number >> HALF)
        told = jnp.where(lane == i, value, told)
    mine = jnp.concatenate([mine_ref[0], told.astype(F32).astype(BF16)], axis=0)
    out_ref[...] = jnp.broadcast_to(mine[None], out_ref.shape)


def fine_dot(first, second):
    parts = []
    for value in (first, second):
        high = value.astype(BF16)
        parts.append((high, (value - high.astype(F32)).astype(BF16)))
    (a, a_rest), (b, b_rest) = parts
    return dot(a, b) + (dot(a, b_rest) + dot(a_rest, b))


def pair_tables_kernel(
    dims, screens_hbm, a_ref, wp_ref, wt_ref, low_ref, wa_ref, screens_ref, sem
):
    facets, height, span, slab, size, columns, local = dims
    rows = facets * height
    copy = pltpu.make_async_copy(screens_hbm, screens_ref, sem)
    copy.start()
    scale = 1.0 / math.sqrt(size)
    w_both = jnp.concatenate(fourier(size, 0, iota((1, span), 1), size, scale), axis=1)
    w_turned = block(*fourier(span, 0, iota((1, size), 1), size, scale), False)
    wt_ref[...] = w_turned.astype(BF16)

    def keep(number, real, imag):
        inside = jnp.broadcast_to((number >= 0) & (number < XC), real.shape)
        zero = jnp.zeros_like(real)
        return jnp.where(inside, real, zero), jnp.where(inside, -imag, zero)

    facet = lax.axis_index("facet")
    lag = STEP * facet
    scale = 1.0 / math.sqrt(slab)
    for f in range(facets):
        lanes = iota((1, span), 1) - STEP * f
        real, imag = keep(lanes, *fourier(slab, 0, lanes, NPAD, scale / math.sqrt(facets)))
        a_ref[f] = block(real.astype(BF16), imag.astype(BF16), False)
    real, imag = fourier(span, -lag, iota((1, slab), 1), NPAD, scale)
    both = fine_dot(w_both, block(*keep(iota(real.shape, 0) - lag, real, imag), False))
    wa_ref[:, :slab] = both[:, :slab].astype(BF16)
    wa_ref[:, slab:] = (-both[:, slab:]).astype(BF16)

    scale = 1.0 / math.sqrt(height)
    row = iota((1, rows), 1)
    behind = STEP * (row >> (height.bit_length() - 1))
    lanes = jnp.broadcast_to(row & (NPAD - 1), (ROWS, rows))
    top = (jnp.broadcast_to(-behind, (ROWS, rows)) + iota((ROWS, rows), 0)) & (NPAD - 1)
    real, imag = ladder(
        wave((top * lanes) & (NPAD - 1), NPAD, scale),
        wave((ROWS * lanes) & (NPAD - 1), NPAD, 1.0),
        span // ROWS,
    )
    both = fine_dot(w_both, block(*keep(iota(real.shape, 0) - behind, real, imag), False)).astype(BF16)
    wp_ref[:size] = both[:, :rows]
    wp_ref[size:] = both[:, rows:]

    pair_rows = 2 * local
    base = facet * height + (lax.axis_index("col") >> 1) * pair_rows
    lanes = iota((1, span), 1) - lag
    real, imag = keep(lanes, *fourier(pair_rows, base, lanes, NPAD, scale))
    both = fine_dot(jnp.concatenate([real, imag], axis=1), w_turned).astype(BF16)
    low_ref[:pair_rows] = both[:, :size]
    low_ref[pair_rows:] = both[:, size:]
    copy.wait()


def dot_nt(first, second):
    return lax.dot_general(first, second, (((1,), (1,)), ((), ())), preferred_element_type=F32)


def pair_kernel(
    dims, x_ref, a_ref, wp_ref, wt_ref, low_ref, wa_ref, screens_ref, mine_ref, other_ref,
    wide_ref, told_ref, numbers_ref, spread_ref, down_ref, half_ref, lifted_ref, seen_ref, gathered_ref, phase_ref, sem,
):
    facets, height, span, slab, size, columns, local = dims
    rows = facets * height
    subgrids = facets
    pair_rows = 2 * local
    mine_columns = columns // 2
    core = lax.axis_index("col") & 1
    base = lax.axis_index("facet") * height + (lax.axis_index("col") >> 1) * pair_rows

    pitch = 2 * (local + 1)
    devices = x_ref.shape[0] // pitch
    wide_ref[...] = x_ref[...].astype(F32)
    told = [
        jnp.concatenate(
            [wide_ref[k * pitch + 2 * local + h : k * pitch + 2 * local + h + 1] for k in range(devices)],
            axis=0,
        )
        for h in (0, 1)
    ]
    told_ref[...] = (told[0] * (1 << HALF) + told[1]).astype(jnp.int32)
    copy = pltpu.make_async_copy(told_ref, numbers_ref, sem)
    copy.start()

    def number(kind, facet, column):
        return numbers_ref[facet * columns + column, kind]

    def spread_number(kind, facet, column, shape):
        own = told_ref[pl.ds(facet * columns + column, 1), :]
        return jnp.broadcast_to(own[:, kind : kind + 1], shape)

    def times(a, b):
        return a[0] * b[0] - a[1] * b[1], a[0] * b[1] + a[1] * b[0]

    def phases(offset, where):
        real, imag = wave((where * offset) & (NPAD - 1), NPAD, 1.0)
        return real, -imag

    own = [
        jnp.concatenate(
            [wide_ref[pl.ds(k * pitch + h, local, stride=2), :] for k in range(devices)], axis=0
        )
        for h in (0, 1)
    ]
    for i in range(mine_columns):
        column = 2 * i + core
        ahead = phases(spread_number(0, 0, column, (ROWS, slab)), iota((ROWS, slab), 1))
        phase_ref[2 * i * ROWS : (2 * i + 1) * ROWS, :] = ahead[0]
        phase_ref[(2 * i + 1) * ROWS : (2 * i + 2) * ROWS, :] = ahead[1]
        line = iota((ROWS, rows), 0)
        offset_rows = jnp.zeros((ROWS, rows), jnp.int32)
        for s in range(subgrids):
            offset_rows = jnp.where(line == s, spread_number(1, s, column, line.shape), offset_rows)
        row_phase = phases(offset_rows, iota((ROWS, rows), 1))
        for h in (0, 1):
            down_ref[i, h, :, :ROWS] = row_phase[h].T
        real, imag = times(
            own,
            [jnp.broadcast_to(p[:1], (rows, slab)) for p in ahead],
        )
        both = jnp.concatenate([real, imag], axis=1)
        turned = both.astype(BF16)
        rest = (both - turned.astype(F32)).astype(BF16)
        for f in range(facets):
            part = slice(f * height, (f + 1) * height)
            spread_ref[i, part, :] = dot(turned[part], a_ref[f]) + dot(rest[part], a_ref[f])

    def lift(i, slot):
        for s in range(subgrids):
            down = [jnp.broadcast_to(down_ref[i, h, :, s : s + 1], (rows, span)) for h in (0, 1)]
            real, imag = times((spread_ref[i, :, :span], spread_ref[i, :, span:]), down)
            lifted_ref[slot, s, :, :span] = real.astype(BF16)
            lifted_ref[slot, s, :, span:] = imag.astype(BF16)

    def halve(slot):
        for s in range(subgrids):
            lifted = lifted_ref[slot, s]
            first = dot(wp_ref[:size], lifted)
            second = dot(wp_ref[size:], lifted)
            part = slice(s * size, (s + 1) * size)
            half_ref[slot, part, :span] = (first[:, :span] - second[:, span:]).astype(BF16)
            half_ref[slot, part, span:] = (first[:, span:] + second[:, :span]).astype(BF16)

    def one_column(i, slot, following):
        if following is not None:
            halve(1 - slot)
        if following is not None and following + 1 < mine_columns:
            lift(following + 1, slot)
        half = half_ref[slot]
        all_real, all_imag = dot(half, wt_ref[:, :size]), dot(half, wt_ref[:, size:])
        for s in range(subgrids):
            part = slice(s * size, (s + 1) * size)
            real, imag = all_real[part], all_imag[part]
            pick = number(2, s, 2 * i + core)
            gain_real, gain_imag = screens_ref[pick, 0], screens_ref[pick, 1]
            seen_ref[slot, s, 0] = (real * gain_real - imag * gain_imag).astype(BF16)
            seen_ref[slot, s, 1] = (real * gain_imag + imag * gain_real).astype(BF16)
        sums = None
        for s in range(subgrids):
            first = dot(low_ref[...], seen_ref[slot, s, 0])
            second = dot(low_ref[...], seen_ref[slot, s, 1])
            real = first[:pair_rows] + second[pair_rows:]
            imag = second[:pair_rows] - first[pair_rows:]
            back = [
                jnp.broadcast_to(down_ref[i, h, pl.ds(base, pair_rows), s : s + 1], (pair_rows, size))
                for h in (0, 1)
            ]
            term = times((real, imag), (back[0], -back[1]))
            sums = term if sums is None else (sums[0] + term[0], sums[1] + term[1])
        part = slice(i * pair_rows, (i + 1) * pair_rows) if isinstance(i, int) else pl.ds(
            pl.multiple_of(i * pair_rows, pair_rows), pair_rows
        )
        gathered_ref[part, :size] = sums[0].astype(BF16)
        gathered_ref[part, size:] = sums[1].astype(BF16)

    lift(0, 0)
    halve(0)
    lift(1, 1)
    copy.wait()
    for i in range(mine_columns):
        one_column(i, i % 2, i + 1 if i + 1 < mine_columns else None)

    first = dot(gathered_ref[:, :size], wa_ref[...])
    second = dot(gathered_ref[:, size:], wa_ref[...])
    real = first[:, :slab] - second[:, slab:]
    imag = first[:, slab:] + second[:, :slab]
    total = None
    for i in range(mine_columns):
        part = slice(i * pair_rows, (i + 1) * pair_rows)
        back_real = jnp.broadcast_to(phase_ref[i * 2 * ROWS : i * 2 * ROWS + 1], (pair_rows, slab))
        back_imag = jnp.broadcast_to(
            phase_ref[i * 2 * ROWS + ROWS : i * 2 * ROWS + ROWS + 1], (pair_rows, slab)
        )
        term = times((real[part], imag[part]), (back_real, -back_imag))
        total = term if total is None else (total[0] + term[0], total[1] + term[1])
    both = jnp.concatenate(total, axis=1)
    mine_ref[...] = jnp.where(core == 0, both[:local], both[local:])
    other_ref[...] = jnp.where(core == 0, both[local:], both[:local])


def pair_body(facets, sub_offsets, col_offsets, screen_index, screens):
    facet_count = lax.axis_size("facet")
    column_count = lax.axis_size("col")
    devices = facet_count * column_count
    local_rows, slab = facets.shape[1], facets.shape[3]
    height = local_rows * column_count
    rows = facet_count * height
    subgrid_count = sub_offsets.shape[1]
    size = screens.shape[2]
    span = -(-(XC + STEP * (facet_count - 1)) // LANES) * LANES
    dims = (facet_count, height, span, slab, size, column_count, local_rows)
    any_space = pl.BlockSpec(memory_space=pl.ANY)
    smem = pl.BlockSpec(memory_space=pltpu.MemorySpace.SMEM)

    outgoing = pl.pallas_call(
        pair_send_kernel,
        out_shape=jax.ShapeDtypeStruct((devices, local_rows + 1, 2, slab), BF16),
        in_specs=[any_space, any_space, smem, smem],
        out_specs=pl.BlockSpec(memory_space=VMEM),
        scratch_shapes=[
            pltpu.VMEM(facets.shape, BF16),
            pltpu.SMEM(sub_offsets.shape, jnp.int32),
            pltpu.SemaphoreType.DMA((2,)),
        ],
        compiler_params=pltpu.CompilerParams(vmem_limit_bytes=VMEM_LIMIT),
        name="send",
    )(in_hbm(facets), in_hbm(sub_offsets), col_offsets, screen_index)
    everyone = lax.all_to_all(
        outgoing, ("facet", "col"), split_axis=0, concat_axis=0, tiled=True
    ).reshape(devices * (local_rows + 1) * 2, slab)
    table_shapes = [
        ((facet_count, 2 * span, 2 * slab), BF16),
        ((2 * size, rows), BF16),
        ((2 * span, 2 * size), BF16),
        ((4 * local_rows, size), BF16),
        ((size, 2 * slab), BF16),
        (screens.shape, F32),
    ]
    table_bytes = sum(math.prod(s) * jnp.dtype(t).itemsize for s, t in table_shapes)
    tables = pl.pallas_call(
        functools.partial(pair_tables_kernel, dims),
        out_shape=[jax.ShapeDtypeStruct(s, t) for s, t in table_shapes],
        in_specs=[any_space],
        out_specs=whole(len(table_shapes)),
        scratch_shapes=[pltpu.SemaphoreType.DMA],
        compiler_params=pltpu.CompilerParams(vmem_limit_bytes=VMEM_LIMIT),
        cost_estimate=pl.CostEstimate(
            flops=100 * table_bytes, bytes_accessed=2 * table_bytes, transcendentals=0
        ),
        name="tables",
    )(in_hbm(screens))
    mine, other = pl.pallas_call(
        functools.partial(pair_kernel, dims),
        out_shape=[jax.ShapeDtypeStruct((local_rows, 2 * slab), F32)] * 2,
        in_specs=whole(1 + len(tables)),
        out_specs=whole(2),
        scratch_shapes=[
            pltpu.VMEM(everyone.shape, F32),
            pltpu.VMEM((devices, slab), jnp.int32),
            pltpu.SMEM((devices, slab), jnp.int32),
            pltpu.VMEM((column_count // 2, rows, 2 * span), F32),
            pltpu.VMEM((column_count // 2, 2, rows, LANES), F32),
            pltpu.VMEM((2, subgrid_count * size, 2 * span), BF16),
            pltpu.VMEM((2, subgrid_count, rows, 2 * span), BF16),
            pltpu.VMEM((2, subgrid_count, 2, size, size), BF16),
            pltpu.VMEM((column_count * local_rows, 2 * size), BF16),
            pltpu.VMEM((column_count * ROWS, slab), F32),
            pltpu.SemaphoreType.DMA,
        ],
        compiler_params=pltpu.CompilerParams(vmem_limit_bytes=VMEM_LIMIT),
        name="window",
    )(everyone, *tables)
    swap = [(i, i ^ 1) for i in range(column_count)]
    summed = mine + lax.ppermute(other, "col", swap)
    return (summed / math.sqrt(column_count * subgrid_count)).reshape(1, local_rows, 2, slab)


def send_kernel(facets_ref, out_ref, mine_ref, sem):
    copy = pltpu.make_async_copy(facets_ref, mine_ref, sem)
    copy.start()
    copy.wait()
    mine = jnp.concatenate([mine_ref[0, :, 0, :], mine_ref[0, :, 1, :]], axis=1)
    out_ref[...] = jnp.broadcast_to(mine[None], out_ref.shape)


def in_hbm(array):
    return pltpu.with_memory_space_constraint(array, pltpu.MemorySpace.HBM)


def whole(count):
    return [pl.BlockSpec(memory_space=VMEM)] * count


def spread_body(facets, sub_offsets, col_offsets, screen_index, screens):
    axes = ("facet", "col")
    facet_count = lax.axis_size("facet")
    column_count = lax.axis_size("col")
    devices = facet_count * column_count
    local_rows, slab = facets.shape[1], facets.shape[3]
    height = local_rows * column_count
    rows = facet_count * height
    subgrid_count = sub_offsets.shape[1]
    owned = subgrid_count // facet_count
    size = screens.shape[2]
    span = -(-(XC + STEP * (facet_count - 1)) // LANES) * LANES
    chunk = max(height, min(rows, CHUNK))
    dims = (facet_count, height, span, slab, size, owned, chunk)

    outgoing = pl.pallas_call(
        send_kernel,
        out_shape=jax.ShapeDtypeStruct((devices, local_rows, 2 * slab), BF16),
        in_specs=[pl.BlockSpec(memory_space=pl.ANY)],
        out_specs=pl.BlockSpec(memory_space=VMEM),
        scratch_shapes=[pltpu.VMEM(facets.shape, BF16), pltpu.SemaphoreType.DMA],
        compiler_params=pltpu.CompilerParams(vmem_limit_bytes=VMEM_LIMIT),
        name="send",
    )(in_hbm(facets))
    everyone = lax.all_to_all(outgoing, axes, split_axis=0, concat_axis=0, tiled=True)
    everyone = everyone.reshape(rows, 2 * slab)
    numbers = jnp.concatenate([col_offsets, screen_index[0], sub_offsets[0]])
    table_shapes = [
        ((facet_count, 2 * slab, 2 * span), BF16),
        ((owned, 2 * size, rows), BF16),
        ((2 * span, 2 * size), BF16),
        ((size, 2 * span), BF16),
        ((owned, rows, 2 * size), BF16),
        ((facet_count, 2 * span, 2 * slab), BF16),
        ((owned, 2, size, size), F32),
    ]
    table_bytes = sum(math.prod(s) * jnp.dtype(t).itemsize for s, t in table_shapes)
    tables = pl.pallas_call(
        functools.partial(tables_kernel, dims),
        out_shape=[jax.ShapeDtypeStruct(s, t) for s, t in table_shapes],
        in_specs=[pl.BlockSpec(memory_space=pl.ANY)] * 2,
        out_specs=whole(len(table_shapes)),
        scratch_shapes=[
            pltpu.SMEM(numbers.shape, jnp.int32),
            pltpu.SemaphoreType.DMA,
            pltpu.SemaphoreType.DMA((owned,)),
        ],
        compiler_params=pltpu.CompilerParams(vmem_limit_bytes=VMEM_LIMIT),
        cost_estimate=pl.CostEstimate(
            flops=100 * table_bytes, bytes_accessed=2 * table_bytes, transcendentals=0
        ),
        name="tables",
    )(numbers, in_hbm(screens))
    terms = pl.pallas_call(
        functools.partial(main_kernel, dims),
        out_shape=jax.ShapeDtypeStruct((rows, 2 * slab), BF16),
        in_specs=whole(1 + len(tables)),
        out_specs=pl.BlockSpec(memory_space=VMEM),
        scratch_shapes=[pltpu.VMEM((rows, 2 * span), BF16)],
        compiler_params=pltpu.CompilerParams(vmem_limit_bytes=VMEM_LIMIT),
        name="window",
    )(everyone, *tables)
    terms = terms.reshape(devices, local_rows, 2 * slab)
    arrived = lax.all_to_all(terms, axes, split_axis=0, concat_axis=0, tiled=True)
    factor = 1.0 / math.sqrt(column_count * subgrid_count)
    summed = jnp.sum(arrived.astype(F32), axis=0) * factor
    return summed.reshape(1, local_rows, 2, slab)


def body(facets, sub_offsets, col_offsets, screen_index, screens):
    columns, subgrids = lax.axis_size("col"), sub_offsets.shape[1]
    alone = columns % 4 == 0 and subgrids == lax.axis_size("facet") and columns * subgrids <= 32
    run = pair_body if alone else spread_body
    return run(facets, sub_offsets, col_offsets, screen_index, screens)


def solution(mesh):
    return jax.shard_map(
        body,
        mesh=mesh,
        in_specs=(P("facet", "col", None, None), P("col", None), P("col"), P("col", "facet"), P()),
        out_specs=P("facet", "col", None, None),
        check_vma=False,
    )
```
